128 devices in a mesh: seq: 4 (over y), grp: 32 (over x, z, core).
Axes of the slice: x: 4, y: 4, z: 4, core: 2. Of those that a mesh axis runs over, the one named last changes fastest.
Arguments:
- basis: bfloat16 [128, 2, 32, 1024], replicated, may hold values from -0.109375 to 0.109375
- background: float32 [32, 4, 2, 2, 32, 1024], P('grp', 'seq'), may hold values from -1.2 to 1.2
- detuning: float32 [32], replicated, may hold values from 1 to 4
- dispersion: float32 [32], replicated, may hold values from 0.5 to 2
- neighbors: int32 [32, 2], replicated, may hold values from 0 to 31, as said below
- step_counts: int32 [32, 4], P('grp', 'seq'), may hold values from 1 to 2
Outputs:
- prefix: float32 [32, 4, 128, 128], P('grp', 'seq')
- monodromy: float32 [128, 128], replicated
The draws below stay inside these ranges and needn't reach their ends.
Inputs may be any that keep to these rules, and one draw needn't show every extreme that they name: `neighbors`: entry (r, k) is cycle r + d or cycle r - d counted around the closed array of 32 cycles, with 1 <= d <= 3; a cycle may be listed twice in one row.
All inputs are finite; a program needn't handle non-finite values.
Results may differ from the reference program's by a relative error of at most 0.0008.
The reference program's roundings to bfloat16 on the way count: a program that leaves them out, or rounds other values in their place, can miss the bound.
Values sent between devices are 32-bit elements; how exact they have to be, the bound alone decides.
A program may use at most 192 MiB of HBM per device.

```python
import math
import jax
import jax.numpy as jnp
from jax import lax

CYCLES = 32
SAMPLES = 1024
BASIS = 128
STEPS = 2
NEIGH = 2
BAND = 3
STATE = 65536
GROUPS = 32
CHAIN = 4


def draw_neighbors(key, part):
    key_dist = jax.random.fold_in(key, 11)
    key_sign = jax.random.fold_in(key, 12)
    distance = jax.random.randint(key_dist, (CYCLES, NEIGH), 1, BAND + 1)
    direction = jax.random.randint(key_sign, (CYCLES, NEIGH), 0, 2) * 2 - 1
    cycle_ids = jnp.arange(CYCLES, dtype=jnp.int32)[:, None]
    return ((cycle_ids + direction * distance) % CYCLES).astype(jnp.int32)


def with_ends(array, key, smallest, largest):
    place = [jax.random.randint(jax.random.fold_in(key, axis), (), 0, length) for axis, length in enumerate(array.shape)]
    main_axis = array.shape.index(max(array.shape))
    beside = place[:main_axis] + [(place[main_axis] + 1) % array.shape[main_axis]] + place[main_axis + 1:]
    return array.at[tuple(place)].set(smallest).at[tuple(beside)].set(largest)


def shard_levels(rng, shape, shards, smallest, largest):
    loudness, own = 1.0, jax.random.fold_in(rng, 6)
    for dim, blocks in shards:
        steps = jnp.exp(jax.random.uniform(jax.random.fold_in(own, dim), (blocks,), jnp.float32, smallest / len(shards), largest / len(shards)))
        loudness = loudness * jnp.repeat(steps, shape[dim] // blocks).reshape([-1 if axis == dim else 1 for axis in range(len(shape))])
    return loudness


def gaussian(stream_key, shape, deviation, most, kind=jnp.bfloat16):
    array = deviation * jax.random.normal(stream_key, shape, jnp.float32)
    return jnp.clip(array, min=-most, max=most).astype(kind)


def setup_inputs(seed: int = 0) -> dict:
    keys = jax.random.split(jax.random.key(seed), 7)
    basis = gaussian(keys[0], (BASIS, 2, CYCLES, SAMPLES), ((STATE * BASIS) ** -0.25), 0.109375)
    background = jnp.clip(jax.random.uniform(keys[1], (GROUPS, CHAIN, STEPS, 2, CYCLES, SAMPLES), jnp.float32, -1.2, 1.2) * shard_levels(keys[1], (GROUPS, CHAIN, STEPS, 2, CYCLES, SAMPLES), ((0, 32), (1, 4)), -0.4, 0.0), -1.2, 1.2)
    detuning = jnp.clip(jax.random.uniform(keys[2], (CYCLES,), jnp.float32, 1.0, 4.0), 1.0, 4.0)
    dispersion = jnp.clip(jnp.exp(jax.random.uniform(keys[3], (CYCLES,), jnp.float32, math.log(0.5), math.log(2.0))), 0.5, 2.0)
    neighbors = draw_neighbors(jax.random.fold_in(keys[6], 71), 0)
    step_counts = with_ends(jax.random.randint(keys[5], (GROUPS, CHAIN), 1, STEPS + 1), jax.random.fold_in(keys[5], 1), 1, STEPS).astype(jnp.int32)
    return dict(basis=basis, background=background, detuning=detuning, dispersion=dispersion, neighbors=neighbors, step_counts=step_counts)


step_size = 0.1
coupling_rate = 1.0
generator_scale = 0.25

def coupling_table(neighbors, cycle_count):
    targets = jnp.arange(cycle_count, dtype=jnp.int32)
    matches = (neighbors[:, :, None] == targets[None, None, :]).astype(jnp.float32)
    return jnp.sum(matches, axis=1)

def propagate(vectors, seg_background, step_total, detuning, dispersion, coupling):
    field_state = vectors
    detune_col = detuning[:, None]
    disp_col = dispersion[:, None]
    for step_index in range(seg_background.shape[0]):
        real_bg = seg_background[step_index, 0]
        imag_bg = seg_background[step_index, 1]
        intensity = 2.0 * (real_bg * real_bg + imag_bg * imag_bg)
        square_re = real_bg * real_bg - imag_bg * imag_bg
        square_im = 2.0 * real_bg * imag_bg
        real_part = field_state[:, 0]
        imag_part = field_state[:, 1]
        lap_re = jnp.roll(real_part, 1, axis=-1) + jnp.roll(real_part, -1, axis=-1) - 2.0 * real_part
        lap_im = jnp.roll(imag_part, 1, axis=-1) + jnp.roll(imag_part, -1, axis=-1) - 2.0 * imag_part
        coupled = jnp.einsum('rm,bcmn->bcrn', coupling, field_state, precision=lax.Precision.HIGHEST)
        real_rate = -real_part + detune_col * imag_part - disp_col * lap_im - intensity * imag_part - square_im * real_part + square_re * imag_part - coupling_rate * coupled[:, 1]
        imag_rate = -imag_part - detune_col * real_part + disp_col * lap_re + intensity * real_part + square_re * real_part + square_im * imag_part + coupling_rate * coupled[:, 0]
        advanced = field_state + step_size * jnp.stack([real_rate, imag_rate], axis=1)
        field_state = jnp.where(step_index < step_total, advanced, field_state)
    return field_state

def cayley(projected):
    generator = generator_scale * (projected - projected.T)
    identity = jnp.eye(projected.shape[0], dtype=jnp.float32)
    plus_gen = identity + generator
    squared = jnp.dot(plus_gen, plus_gen, precision=lax.Precision.HIGHEST)
    normal = identity + jnp.dot(generator.T, generator, precision=lax.Precision.HIGHEST)
    factor = jnp.linalg.cholesky(normal)
    return jax.scipy.linalg.cho_solve((factor, True), squared)

def reference(basis, background, detuning, dispersion, neighbors, step_counts):
    coupling = coupling_table(neighbors, CYCLES)
    vectors = basis.astype(jnp.float32)
    flat_basis = vectors.reshape(BASIS, STATE)
    flat_background = background.reshape(GROUPS * CHAIN, STEPS, 2, CYCLES, SAMPLES)
    totals = step_counts.reshape(GROUPS * CHAIN)

    def one_segment(operands):
        seg_background, step_total = operands
        field_state = propagate(vectors, seg_background, step_total, detuning, dispersion, coupling)
        rounded = lax.optimization_barrier(field_state.astype(jnp.bfloat16)).astype(jnp.float32)
        projected = jnp.dot(flat_basis, rounded.reshape(BASIS, STATE).T, precision=lax.Precision.HIGHEST)
        return cayley(projected)
    transfers = lax.map(one_segment, (flat_background, totals))

    def advance(product, factor_mat):
        return (jnp.dot(factor_mat, product, precision=lax.Precision.HIGHEST), product)
    start = jnp.eye(BASIS, dtype=jnp.float32)
    monodromy, prefixes = lax.scan(advance, start, transfers)
    return (prefixes.reshape(GROUPS, CHAIN, BASIS, BASIS), monodromy)
```

```python
import jax
import jax.numpy as jnp
from jax import lax
from jax.experimental import pallas as pl
from jax.experimental.pallas import tpu as pltpu
from jax.sharding import PartitionSpec as P

HI = lax.Precision.HIGHEST
GROUP = 16


def split3(x):
    hi = x.astype(jnp.bfloat16)
    rest = x - hi.astype(jnp.float32)
    mid = rest.astype(jnp.bfloat16)
    low = (rest - mid.astype(jnp.float32)).astype(jnp.bfloat16)
    return hi, mid, low


def left6(x):
    h, m, l = split3(x)
    return jnp.concatenate([h, h, m, m, h, l], axis=1)


def right6(x):
    h, m, l = split3(x)
    return jnp.concatenate([h, m, h, m, l, h], axis=0)


def mm(a, b):
    return jnp.dot(left6(a), right6(b), preferred_element_type=jnp.float32)


def _transfer_kernel(nbr, steps, det, disp, basis, bg, out, perm, co, w0, w1, bc, pr, acc):
    g = pl.program_id(0)
    last = pl.num_programs(0) - 1
    vecs, cycles, samples = bc.shape[2], bc.shape[1], bc.shape[3]

    @pl.when(g == 0)
    def _():
        i = lax.broadcasted_iota(jnp.int32, (256, 256), 0)
        j = lax.broadcasted_iota(jnp.int32, (256, 256), 1)
        hit = jnp.logical_and(i // 16 == j % 16, i % 16 == j // 16)
        perm[...] = jnp.where(hit, 1.0, 0.0).astype(jnp.bfloat16)

        @pl.loop(0, cycles)
        def _(r):
            for t in range(2):
                a = bg[t, 0, pl.ds(r, 1), :]
                b = bg[t, 1, pl.ds(r, 1), :]
                inten = 2.0 * (a * a + b * b)
                p = a * a - b * b
                q = 2.0 * a * b
                lin = (det[r] + 2.0 * disp[r]) - inten
                for k, val in enumerate((9.0 - q, lin + p, 9.0 + q, p - lin)):
                    co[t, k, r] = jnp.broadcast_to(val, (8, samples))

    for p in range(2):
        for h in range(cycles // 16):
            for nb in range(samples // 256):
                x = basis[:, p, h * 16:(h + 1) * 16, nb * 256:(nb + 1) * 256].reshape(256, 256)
                y = jnp.dot(perm[...], x, preferred_element_type=jnp.float32).reshape(16, 16, 256)
                w0[p, h * 16:(h + 1) * 16, :, nb * 256:(nb + 1) * 256] = y
                bc[p, h * 16:(h + 1) * 16, pl.ds(g * GROUP, GROUP), nb * 256:(nb + 1) * 256] = y.astype(jnp.bfloat16)

    def advance(src, t, r, lo):
        n0, n1 = nbr[r, 0], nbr[r, 1]
        vs = slice(lo, lo + 8)
        beta = disp[r]
        u, v = src[0, r, vs, :], src[1, r, vs, :]
        cu = src[0, n0, vs, :] + src[0, n1, vs, :]
        cv = src[1, n0, vs, :] + src[1, n1, vs, :]
        su = pltpu.roll(u, 1, 1) + pltpu.roll(u, samples - 1, 1)
        sv = pltpu.roll(v, 1, 1) + pltpu.roll(v, samples - 1, 1)
        nu = (co[t, 0, r] * u + co[t, 1, r] * v) - (beta * sv + cv)
        nv = (co[t, 2, r] * v + co[t, 3, r] * u) + (beta * su + cu)
        return nu, nv

    @pl.loop(0, cycles)
    def _(r):
        for lo in range(0, GROUP, 8):
            nu, nv = advance(w0, 0, r, lo)
            w1[0, r, lo:lo + 8, :] = nu
            w1[1, r, lo:lo + 8, :] = nv

    rows = pl.ds(pl.multiple_of(g * GROUP, GROUP), GROUP)

    @pl.when(steps[0] >= 2)
    def _():
        @pl.loop(0, cycles)
        def _(r):
            res = [advance(w1, 1, r, lo) for lo in range(0, GROUP, 8)]
            for p in range(2):
                full = jnp.concatenate([0.01 * x[p] for x in res], axis=0)
                pr[p, r, rows, :] = full.astype(jnp.bfloat16)

    @pl.when(steps[0] < 2)
    def _():
        @pl.loop(0, cycles)
        def _(r):
            for p in range(2):
                pr[p, r, rows, :] = (0.1 * w1[p, r]).astype(jnp.bfloat16)

    @pl.when(g == last)
    def _():
        acc[...] = jnp.zeros_like(acc)

        @pl.loop(0, cycles)
        def _(r):
            tot = acc[...]
            for p in range(2):
                tot += lax.dot_general(bc[p, r], pr[p, r], (((1,), (1,)), ((), ())),
                                       preferred_element_type=jnp.float32)
            acc[...] = tot

        proj = acc[...]
        gen = 0.25 * (proj - proj.T)
        i = lax.broadcasted_iota(jnp.int32, (vecs, vecs), 0)
        j = lax.broadcasted_iota(jnp.int32, (vecs, vecs), 1)
        eye = jnp.where(i == j, 1.0, 0.0)
        gram = -mm(gen, gen)
        bound = jnp.max(jnp.sum(jnp.abs(gram), axis=0))
        scale = 2.0 / (2.0 + bound)
        resid = eye - scale * (eye + gram)
        prod = scale * (eye + 2.0 * gen - gram)

        def more(c):
            return c[0] > 1e-7

        def body(c):
            rho, rs, pd = c
            return (rho * rho,
                    mm(rs, rs),
                    pd + mm(rs, pd))

        out[...] = lax.while_loop(more, body, (0.5 * bound * scale, resid, prod))[2]


def segment_transfer(basis, bg, det, disp, nbr, steps):
    vecs, _, cycles, samples = basis.shape
    smem = pl.BlockSpec(memory_space=pltpu.SMEM)
    return pl.pallas_call(
        _transfer_kernel,
        grid=(vecs // GROUP,),
        out_shape=jax.ShapeDtypeStruct((vecs, vecs), jnp.float32),
        in_specs=[smem, smem, smem, smem,
                  pl.BlockSpec((GROUP, 2, cycles, samples), lambda g: (g, 0, 0, 0)),
                  pl.BlockSpec(memory_space=pltpu.VMEM)],
        out_specs=pl.BlockSpec((vecs, vecs), lambda g: (0, 0)),
        scratch_shapes=[
            pltpu.VMEM((256, 256), jnp.bfloat16),
            pltpu.VMEM((2, 4, cycles, 8, samples), jnp.float32),
            pltpu.VMEM((2, cycles, GROUP, samples), jnp.float32),
            pltpu.VMEM((2, cycles, GROUP, samples), jnp.float32),
            pltpu.VMEM((2, cycles, vecs, samples), jnp.bfloat16),
            pltpu.VMEM((2, cycles, vecs, samples), jnp.bfloat16),
            pltpu.VMEM((vecs, vecs), jnp.float32),
        ],
        compiler_params=pltpu.CompilerParams(vmem_limit_bytes=60 * 1024 * 1024),
        name="segment_transfer",
    )(nbr, steps, det, disp, basis, bg)


def shifted_2(value, axis, steps):
    count = lax.axis_size(axis)
    first, last = (max(0, -steps), min(count, count - steps))
    return lax.ppermute(value, axis, [(source, source + steps) for source in range(first, last)])


def broadcast(x, axis, root):
    mine = lax.axis_index(axis) == root
    return lax.psum(jnp.where(mine, x, jnp.zeros_like(x)), axis)


def compose(latter, former):
    return jnp.dot(latter, former, precision=lax.Precision.HIGHEST)


def batch_compose(former, latter):
    return jnp.einsum("bij,bjk->bik", latter, former, precision=lax.Precision.HIGHEST)


def shards(basis, background, detuning, dispersion, neighbors, step_counts):
    vec_count = basis.shape[0]
    transfer = segment_transfer(
        basis, background[0, 0], detuning, dispersion, neighbors, step_counts.reshape(1)
    )
    identity = jnp.eye(vec_count, dtype=jnp.float32)
    seq_count = lax.axis_size("seq")
    seq_pos = lax.axis_index("seq")
    before = identity
    through = transfer
    for hop_index in range(1, seq_count):
        arrived = shifted_2(through, "seq", 1)
        is_mine = seq_pos == hop_index
        before = jnp.where(is_mine, arrived, before)
        through = jnp.where(is_mine, compose(transfer, arrived), through)
    group_product = broadcast(through, "seq", seq_count - 1)
    grp_count = lax.axis_size("grp")
    grp_pos = lax.axis_index("grp")
    totals = lax.all_gather(group_product[None], "grp", axis=0, tiled=True)
    running = lax.associative_scan(batch_compose, totals)
    monodromy = running[grp_count - 1]
    shifted = jnp.concatenate([identity[None], running[:-1]], axis=0)
    earlier = lax.dynamic_index_in_dim(shifted, grp_pos, 0, keepdims=False)
    prefix = compose(before, earlier)
    return (prefix[None, None], monodromy)


def solution(mesh):
    in_specs = (P(), P("grp", "seq", None, None, None, None), P(), P(), P(), P("grp", "seq"))
    out_specs = (P("grp", "seq", None, None), P())
    return jax.shard_map(shards, mesh=mesh, in_specs=in_specs, out_specs=out_specs, check_vma=False)
```

```python
import functools
import jax
import jax.numpy as jnp
from jax import lax
from jax.experimental import pallas as pl
from jax.experimental.pallas import tpu as pltpu
from jax.sharding import PartitionSpec as P

HI = lax.Precision.HIGHEST
GROUP = 16


def split3(x):
    hi = x.astype(jnp.bfloat16)
    rest = x - hi.astype(jnp.float32)
    mid = rest.astype(jnp.bfloat16)
    low = (rest - mid.astype(jnp.float32)).astype(jnp.bfloat16)
    return hi, mid, low


def left6(x):
    h, m, l = split3(x)
    return jnp.concatenate([h, h, m, m, h, l], axis=1)


def right6(x):
    h, m, l = split3(x)
    return jnp.concatenate([h, m, h, m, l, h], axis=0)


def mm(a, b):
    return jnp.dot(left6(a), right6(b), preferred_element_type=jnp.float32)


def _transfer_kernel(nbr, steps, det, disp, basis, bg, out, perm, co, w0, w1, bc, pr, acc):
    g = pl.program_id(0)
    last = pl.num_programs(0) - 1
    vecs, cycles, samples = bc.shape[2], bc.shape[1], bc.shape[3]

    @pl.when(g == 0)
    def _():
        i = lax.broadcasted_iota(jnp.int32, (256, 256), 0)
        j = lax.broadcasted_iota(jnp.int32, (256, 256), 1)
        hit = jnp.logical_and(i // 16 == j % 16, i % 16 == j // 16)
        perm[...] = jnp.where(hit, 1.0, 0.0).astype(jnp.bfloat16)

        @pl.loop(0, cycles)
        def _(r):
            for t in range(2):
                a = bg[t, 0, pl.ds(r, 1), :]
                b = bg[t, 1, pl.ds(r, 1), :]
                inten = 2.0 * (a * a + b * b)
                p = a * a - b * b
                q = 2.0 * a * b
                lin = (det[r] + 2.0 * disp[r]) - inten
                for k, val in enumerate((9.0 - q, lin + p, 9.0 + q, p - lin)):
                    co[t, k, r] = jnp.broadcast_to(val, (8, samples))

    for p in range(2):
        for h in range(cycles // 16):
            for nb in range(samples // 256):
                x = basis[:, p, h * 16:(h + 1) * 16, nb * 256:(nb + 1) * 256].reshape(256, 256)
                y = jnp.dot(perm[...], x, preferred_element_type=jnp.float32).reshape(16, 16, 256)
                w0[p, h * 16:(h + 1) * 16, :, nb * 256:(nb + 1) * 256] = y
                bc[p, h * 16:(h + 1) * 16, pl.ds(g * GROUP, GROUP), nb * 256:(nb + 1) * 256] = y.astype(jnp.bfloat16)

    def advance(src, t, r, lo):
        n0, n1 = nbr[r, 0], nbr[r, 1]
        vs = slice(lo, lo + 8)
        beta = disp[r]
        u, v = src[0, r, vs, :], src[1, r, vs, :]
        cu = src[0, n0, vs, :] + src[0, n1, vs, :]
        cv = src[1, n0, vs, :] + src[1, n1, vs, :]
        su = pltpu.roll(u, 1, 1) + pltpu.roll(u, samples - 1, 1)
        sv = pltpu.roll(v, 1, 1) + pltpu.roll(v, samples - 1, 1)
        nu = (co[t, 0, r] * u + co[t, 1, r] * v) - (beta * sv + cv)
        nv = (co[t, 2, r] * v + co[t, 3, r] * u) + (beta * su + cu)
        return nu, nv

    @pl.loop(0, cycles)
    def _(r):
        for lo in range(0, GROUP, 8):
            nu, nv = advance(w0, 0, r, lo)
            w1[0, r, lo:lo + 8, :] = nu
            w1[1, r, lo:lo + 8, :] = nv

    rows = pl.ds(pl.multiple_of(g * GROUP, GROUP), GROUP)

    @pl.when(steps[0] >= 2)
    def _():
        @pl.loop(0, cycles)
        def _(r):
            res = [advance(w1, 1, r, lo) for lo in range(0, GROUP, 8)]
            for p in range(2):
                full = jnp.concatenate([0.01 * x[p] for x in res], axis=0)
                pr[p, r, rows, :] = full.astype(jnp.bfloat16)

    @pl.when(steps[0] < 2)
    def _():
        @pl.loop(0, cycles)
        def _(r):
            for p in range(2):
                pr[p, r, rows, :] = (0.1 * w1[p, r]).astype(jnp.bfloat16)

    @pl.when(g == last)
    def _():
        acc[...] = jnp.zeros_like(acc)

        @pl.loop(0, cycles)
        def _(r):
            tot = acc[...]
            for p in range(2):
                tot += lax.dot_general(bc[p, r], pr[p, r], (((1,), (1,)), ((), ())),
                                       preferred_element_type=jnp.float32)
            acc[...] = tot

        proj = acc[...]
        gen = 0.25 * (proj - proj.T)
        i = lax.broadcasted_iota(jnp.int32, (vecs, vecs), 0)
        j = lax.broadcasted_iota(jnp.int32, (vecs, vecs), 1)
        eye = jnp.where(i == j, 1.0, 0.0)
        gram = -mm(gen, gen)
        bound = jnp.max(jnp.sum(jnp.abs(gram), axis=0))
        scale = 2.0 / (2.0 + bound)
        resid = eye - scale * (eye + gram)
        prod = scale * (eye + 2.0 * gen - gram)

        def more(c):
            return c[0] > 1e-7

        def body(c):
            rho, rs, pd = c
            return (rho * rho,
                    mm(rs, rs),
                    pd + mm(rs, pd))

        out[...] = lax.while_loop(more, body, (0.5 * bound * scale, resid, prod))[2]


def segment_transfer(basis, bg, det, disp, nbr, steps):
    vecs, _, cycles, samples = basis.shape
    smem = pl.BlockSpec(memory_space=pltpu.SMEM)
    return pl.pallas_call(
        _transfer_kernel,
        grid=(vecs // GROUP,),
        out_shape=jax.ShapeDtypeStruct((vecs, vecs), jnp.float32),
        in_specs=[smem, smem, smem, smem,
                  pl.BlockSpec((GROUP, 2, cycles, samples), lambda g: (g, 0, 0, 0)),
                  pl.BlockSpec(memory_space=pltpu.VMEM)],
        out_specs=pl.BlockSpec((vecs, vecs), lambda g: (0, 0)),
        scratch_shapes=[
            pltpu.VMEM((256, 256), jnp.bfloat16),
            pltpu.VMEM((2, 4, cycles, 8, samples), jnp.float32),
            pltpu.VMEM((2, cycles, GROUP, samples), jnp.float32),
            pltpu.VMEM((2, cycles, GROUP, samples), jnp.float32),
            pltpu.VMEM((2, cycles, vecs, samples), jnp.bfloat16),
            pltpu.VMEM((2, cycles, vecs, samples), jnp.bfloat16),
            pltpu.VMEM((vecs, vecs), jnp.float32),
        ],
        compiler_params=pltpu.CompilerParams(vmem_limit_bytes=60 * 1024 * 1024),
        name="segment_transfer",
    )(nbr, steps, det, disp, basis, bg)


def split2(x):
    hi = x.astype(jnp.bfloat16)
    return hi, (x - hi.astype(jnp.float32)).astype(jnp.bfloat16)


def mm3(a, b):
    ah, al = split2(a)
    bh, bl = split2(b)
    return jnp.dot(jnp.concatenate([ah, ah, al], axis=1), jnp.concatenate([bh, bl, bh], axis=0),
                   preferred_element_type=jnp.float32)


def _chain_kernel(t_ref, pre_ref, mono_ref, slots, pair, low, before, send_sem, recv_sem):
    seq, grp = lax.axis_index("seq"), lax.axis_index("grp")
    core = lax.rem(grp, 2)
    depth = lax.rem(lax.div(grp, 2), 4)
    wide = lax.div(grp, 8)
    rounds = (
        (4, seq, lambda pos: (pos, grp)),
        (2, core, lambda pos: (seq, grp - core + pos)),
        (4, depth, lambda pos: (seq, grp + (pos - depth) * 2)),
        (4, wide, lambda pos: (seq, grp + (pos - wide) * 8)),
    )
    mesh_id = pl.DeviceIdType.MESH
    barrier = pltpu.get_barrier_semaphore()
    for radix, pos, place in rounds:
        for hop in range(1, radix):
            pl.semaphore_signal(barrier, inc=1, device_id=place(lax.rem(pos + hop, radix)), device_id_type=mesh_id)
    pl.semaphore_wait(barrier, sum(r[0] - 1 for r in rounds))

    def prefix_step(k, last):
        radix, pos, _ = rounds[k]

        @pl.when(pos == 1)
        def _():
            before[...] = slots[k, 0] if k == 0 else mm3(before[...], slots[k, 0])

        if radix == 4:
            @pl.when(pos == 2)
            def _():
                before[...] = low[...] if k == 0 else mm3(before[...], low[...])

            @pl.when(pos == 3)
            def _():
                left = slots[k, 2] if k == 0 else mm3(before[...], slots[k, 2])
                before[...] = mm3(left, low[...])

    n = t_ref.shape[0]
    i = lax.broadcasted_iota(jnp.int32, (n, n), 0)
    j = lax.broadcasted_iota(jnp.int32, (n, n), 1)
    before[...] = jnp.where(i == j, 1.0, 0.0)
    sends = []
    own = t_ref
    for k, (radix, pos, place) in enumerate(rounds):
        copies = []
        for hop in ((2, 1, 3) if radix == 4 else (1,)):
            copy = pltpu.make_async_remote_copy(
                src_ref=own, dst_ref=slots.at[k, pos], send_sem=send_sem.at[k, hop], recv_sem=recv_sem.at[k, hop],
                device_id=place(lax.rem(pos + hop, radix)), device_id_type=mesh_id)
            copy.start()
            copies.append(copy)
        sends += copies
        slots[k, pos] = own[...]
        if k:
            prefix_step(k - 1, False)
        for copy in copies:
            copy.wait_recv()
        if radix == 4:
            first = mm3(slots[k, 1], slots[k, 0])
            low[...] = first
            total = mm3(mm3(slots[k, 3], slots[k, 2]), first)
        else:
            total = mm3(slots[k, 1], slots[k, 0])
        if k + 1 < len(rounds):
            pair[k] = total
            own = pair.at[k]
        else:
            mono_ref[...] = total
    prefix_step(len(rounds) - 1, True)
    pre_ref[...] = before[...]
    for copy in sends:
        copy.wait_send()


def chain(t):
    n = t.shape[0]
    shape = jax.ShapeDtypeStruct((n, n), jnp.float32)
    vm = pl.BlockSpec(memory_space=pltpu.VMEM)
    return pl.pallas_call(
        _chain_kernel, out_shape=(shape, shape), in_specs=[vm], out_specs=(vm, vm),
        scratch_shapes=[pltpu.VMEM((4, 4, n, n), jnp.float32), pltpu.VMEM((3, n, n), jnp.float32),
                        pltpu.VMEM((n, n), jnp.float32), pltpu.VMEM((n, n), jnp.float32),
                        pltpu.SemaphoreType.DMA((4, 4)), pltpu.SemaphoreType.DMA((4, 4))],
        compiler_params=pltpu.CompilerParams(collective_id=0, has_side_effects=True),
        name="chain_products")(t)

def shards(basis, background, detuning, dispersion, neighbors, step_counts):
    own = segment_transfer(
        basis, background[0, 0], detuning, dispersion, neighbors, step_counts.reshape(1)
    )
    prefix, monodromy = chain(own)
    return (prefix[None, None], monodromy)


def solution(mesh):
    in_specs = (P(), P("grp", "seq", None, None, None, None), P(), P(), P(), P("grp", "seq"))
    out_specs = (P("grp", "seq", None, None), P())
    return jax.shard_map(shards, mesh=mesh, in_specs=in_specs, out_specs=out_specs, check_vma=False)
```

```python
import functools
import jax
import jax.numpy as jnp
from jax import lax
from jax.experimental import pallas as pl
from jax.experimental.pallas import tpu as pltpu
from jax.sharding import PartitionSpec as P

HI = lax.Precision.HIGHEST
GROUP = 16


def split3(x):
    hi = x.astype(jnp.bfloat16)
    rest = x - hi.astype(jnp.float32)
    mid = rest.astype(jnp.bfloat16)
    low = (rest - mid.astype(jnp.float32)).astype(jnp.bfloat16)
    return hi, mid, low


def left6(x):
    h, m, l = split3(x)
    return jnp.concatenate([h, h, m, m, h, l], axis=1)


def right6(x):
    h, m, l = split3(x)
    return jnp.concatenate([h, m, h, m, l, h], axis=0)


def mm(a, b):
    return jnp.dot(left6(a), right6(b), preferred_element_type=jnp.float32)


def _transfer_kernel(nbr, steps, det, disp, basis, bg, out, perm, co, w0, w1, bc, pr, acc):
    g = pl.program_id(0)
    last = pl.num_programs(0) - 1
    vecs, cycles, samples = bc.shape[2], bc.shape[1], bc.shape[3]

    @pl.when(g == 0)
    def _():
        i = lax.broadcasted_iota(jnp.int32, (256, 256), 0)
        j = lax.broadcasted_iota(jnp.int32, (256, 256), 1)
        hit = jnp.logical_and(i // 16 == j % 16, i % 16 == j // 16)
        perm[...] = jnp.where(hit, 1.0, 0.0).astype(jnp.bfloat16)

        @pl.loop(0, cycles)
        def _(r):
            for t in range(2):
                a = bg[t, 0, pl.ds(r, 1), :]
                b = bg[t, 1, pl.ds(r, 1), :]
                inten = 2.0 * (a * a + b * b)
                p = a * a - b * b
                q = 2.0 * a * b
                lin = (det[r] + 2.0 * disp[r]) - inten
                for k, val in enumerate((9.0 - q, lin + p, 9.0 + q, p - lin)):
                    co[t, k, r] = jnp.broadcast_to(val, (8, samples))

    for p in range(2):
        for h in range(cycles // 16):
            for nb in range(samples // 256):
                x = basis[:, p, h * 16:(h + 1) * 16, nb * 256:(nb + 1) * 256].reshape(256, 256)
                y = jnp.dot(perm[...], x, preferred_element_type=jnp.float32).reshape(16, 16, 256)
                w0[p, h * 16:(h + 1) * 16, :, nb * 256:(nb + 1) * 256] = y
                bc[p, h * 16:(h + 1) * 16, pl.ds(g * GROUP, GROUP), nb * 256:(nb + 1) * 256] = y.astype(jnp.bfloat16)

    def around(x):
        lane = lax.broadcasted_iota(jnp.int32, (8, 128), 1)
        first, final = lane == 0, lane == 127
        cols = [x[:, 128 * j:128 * j + 128] for j in range(samples // 128)]
        n = len(cols)
        down = [pltpu.roll(c, 1, 1) for c in cols]
        up = [pltpu.roll(c, 127, 1) for c in cols]
        return jnp.concatenate([jnp.where(first, down[j - 1], down[j]) + jnp.where(final, up[(j + 1) % n], up[j]) for j in range(n)], axis=1)

    def advance(src, t, r, lo):
        n0, n1 = nbr[0, r], nbr[1, r]
        vs = slice(lo, lo + 8)
        beta = disp[r]
        u, v = src[0, r, vs, :], src[1, r, vs, :]
        cu = src[0, n0, vs, :] + src[0, n1, vs, :]
        cv = src[1, n0, vs, :] + src[1, n1, vs, :]
        su = around(u)
        sv = around(v)
        nu = (co[t, 0, r] * u + co[t, 1, r] * v) - (beta * sv + cv)
        nv = (co[t, 2, r] * v + co[t, 3, r] * u) + (beta * su + cu)
        return nu, nv

    @pl.loop(0, cycles // 8)
    def _(rr):
        for r in [rr * 8 + k for k in range(8)]:
            for lo in range(0, GROUP, 8):
                nu, nv = advance(w0, 0, r, lo)
                w1[0, r, lo:lo + 8, :] = nu
                w1[1, r, lo:lo + 8, :] = nv

    rows = pl.ds(pl.multiple_of(g * GROUP, GROUP), GROUP)

    @pl.when(steps[0] >= 2)
    def _():
        @pl.loop(0, cycles // 8)
        def _(rr):
            for r in [rr * 8 + k for k in range(8)]:
                res = [advance(w1, 1, r, lo) for lo in range(0, GROUP, 8)]
                for p in range(2):
                    full = jnp.concatenate([0.01 * x[p] for x in res], axis=0)
                    pr[p, r, rows, :] = full.astype(jnp.bfloat16)

    @pl.when(steps[0] < 2)
    def _():
        @pl.loop(0, cycles)
        def _(r):
            for p in range(2):
                pr[p, r, rows, :] = (0.1 * w1[p, r]).astype(jnp.bfloat16)

    @pl.when(g == last)
    def _():
        acc[...] = jnp.zeros_like(acc)

        @pl.loop(0, cycles)
        def _(r):
            tot = acc[...]
            for p in range(2):
                tot += lax.dot_general(bc[p, r], pr[p, r], (((1,), (1,)), ((), ())),
                                       preferred_element_type=jnp.float32)
            acc[...] = tot

        proj = acc[...]
        gen = 0.25 * (proj - proj.T)
        i = lax.broadcasted_iota(jnp.int32, (vecs, vecs), 0)
        j = lax.broadcasted_iota(jnp.int32, (vecs, vecs), 1)
        eye = jnp.where(i == j, 1.0, 0.0)
        gram = -mm(gen, gen)
        bound = jnp.max(jnp.sum(jnp.abs(gram), axis=0))
        scale = 2.0 / (2.0 + bound)
        resid = eye - scale * (eye + gram)
        prod = scale * (eye + 2.0 * gen - gram)

        def more(c):
            return c[0] > 1e-7

        def body(c):
            rho, rs, pd = c
            return (rho * rho,
                    mm(rs, rs),
                    pd + mm(rs, pd))

        out[...] = lax.while_loop(more, body, (0.5 * bound * scale, resid, prod))[2]


def segment_transfer(basis, bg, det, disp, nbr, steps):
    vecs, _, cycles, samples = basis.shape
    smem = pl.BlockSpec(memory_space=pltpu.SMEM)
    return pl.pallas_call(
        _transfer_kernel,
        grid=(vecs // GROUP,),
        out_shape=jax.ShapeDtypeStruct((vecs, vecs), jnp.float32),
        in_specs=[smem, smem, smem, smem,
                  pl.BlockSpec((GROUP, 2, cycles, samples), lambda g: (g, 0, 0, 0)),
                  pl.BlockSpec(memory_space=pltpu.VMEM)],
        out_specs=pl.BlockSpec((vecs, vecs), lambda g: (0, 0)),
        scratch_shapes=[
            pltpu.VMEM((256, 256), jnp.bfloat16),
            pltpu.VMEM((2, 4, cycles, 8, samples), jnp.float32),
            pltpu.VMEM((2, cycles, GROUP, samples), jnp.float32),
            pltpu.VMEM((2, cycles, GROUP, samples), jnp.float32),
            pltpu.VMEM((2, cycles, vecs, samples), jnp.bfloat16),
            pltpu.VMEM((2, cycles, vecs, samples), jnp.bfloat16),
            pltpu.VMEM((vecs, vecs), jnp.float32),
        ],
        compiler_params=pltpu.CompilerParams(vmem_limit_bytes=60 * 1024 * 1024),
        name="segment_transfer",
    )(nbr.T, steps, det, disp, basis, bg)


def split2(x):
    hi = x.astype(jnp.bfloat16)
    return hi, (x - hi.astype(jnp.float32)).astype(jnp.bfloat16)


def mm3(a, b):
    ah, al = split2(a)
    bh, bl = split2(b)
    return jnp.dot(jnp.concatenate([ah, ah, al], axis=1), jnp.concatenate([bh, bl, bh], axis=0),
                   preferred_element_type=jnp.float32)


def _chain_kernel(t_ref, pre_ref, mono_ref, slots, pair, low, before, send_sem, recv_sem):
    seq, grp = lax.axis_index("seq"), lax.axis_index("grp")
    core = lax.rem(grp, 2)
    depth = lax.rem(lax.div(grp, 2), 4)
    wide = lax.div(grp, 8)
    rounds = (
        (4, seq, lambda pos: (pos, grp)),
        (2, core, lambda pos: (seq, grp - core + pos)),
        (4, depth, lambda pos: (seq, grp + (pos - depth) * 2)),
        (4, wide, lambda pos: (seq, grp + (pos - wide) * 8)),
    )
    mesh_id = pl.DeviceIdType.MESH
    barrier = pltpu.get_barrier_semaphore()
    for radix, pos, place in rounds:
        for hop in range(1, radix):
            pl.semaphore_signal(barrier, inc=1, device_id=place(lax.rem(pos + hop, radix)), device_id_type=mesh_id)
    pl.semaphore_wait(barrier, sum(r[0] - 1 for r in rounds))

    def prefix_step(k, last):
        radix, pos, _ = rounds[k]

        @pl.when(pos == 1)
        def _():
            before[...] = slots[k, 0] if k == 0 else mm3(before[...], slots[k, 0])

        if radix == 4:
            @pl.when(pos == 2)
            def _():
                before[...] = low[...] if k == 0 else mm3(before[...], low[...])

            @pl.when(pos == 3)
            def _():
                left = slots[k, 2] if k == 0 else mm3(before[...], slots[k, 2])
                before[...] = mm3(left, low[...])

    n = t_ref.shape[0]
    i = lax.broadcasted_iota(jnp.int32, (n, n), 0)
    j = lax.broadcasted_iota(jnp.int32, (n, n), 1)
    before[...] = jnp.where(i == j, 1.0, 0.0)
    sends = []
    own = t_ref
    for k, (radix, pos, place) in enumerate(rounds):
        copies = []
        for hop in ((2, 1, 3) if radix == 4 else (1,)):
            copy = pltpu.make_async_remote_copy(
                src_ref=own, dst_ref=slots.at[k, pos], send_sem=send_sem.at[k, hop], recv_sem=recv_sem.at[k, hop],
                device_id=place(lax.rem(pos + hop, radix)), device_id_type=mesh_id)
            copy.start()
            copies.append(copy)
        sends += copies
        slots[k, pos] = own[...]
        if k:
            prefix_step(k - 1, False)
        for copy in copies:
            copy.wait_recv()
        if radix == 4:
            first = mm3(slots[k, 1], slots[k, 0])
            low[...] = first
            total = mm3(mm3(slots[k, 3], slots[k, 2]), first)
        else:
            total = mm3(slots[k, 1], slots[k, 0])
        if k + 1 < len(rounds):
            pair[k] = total
            own = pair.at[k]
        else:
            mono_ref[...] = total
    prefix_step(len(rounds) - 1, True)
    pre_ref[...] = before[...]
    for copy in sends:
        copy.wait_send()


def chain(t):
    n = t.shape[0]
    shape = jax.ShapeDtypeStruct((n, n), jnp.float32)
    vm = pl.BlockSpec(memory_space=pltpu.VMEM)
    return pl.pallas_call(
        _chain_kernel, out_shape=(shape, shape), in_specs=[vm], out_specs=(vm, vm),
        scratch_shapes=[pltpu.VMEM((4, 4, n, n), jnp.float32), pltpu.VMEM((3, n, n), jnp.float32),
                        pltpu.VMEM((n, n), jnp.float32), pltpu.VMEM((n, n), jnp.float32),
                        pltpu.SemaphoreType.DMA((4, 4)), pltpu.SemaphoreType.DMA((4, 4))],
        compiler_params=pltpu.CompilerParams(collective_id=0, has_side_effects=True),
        name="chain_products")(t)

def shards(basis, background, detuning, dispersion, neighbors, step_counts):
    own = segment_transfer(
        basis, background[0, 0], detuning, dispersion, neighbors, step_counts.reshape(1)
    )
    prefix, monodromy = chain(own)
    return (prefix[None, None], monodromy)


def solution(mesh):
    in_specs = (P(), P("grp", "seq", None, None, None, None), P(), P(), P(), P("grp", "seq"))
    out_specs = (P("grp", "seq", None, None), P())
    return jax.shard_map(shards, mesh=mesh, in_specs=in_specs, out_specs=out_specs, check_vma=False)
```

```python
import functools
import jax
import jax.numpy as jnp
from jax import lax
from jax.experimental import pallas as pl
from jax.experimental.pallas import tpu as pltpu
from jax.sharding import PartitionSpec as P

GROUP = 16
UNROLL = 16
F32, BF16 = jnp.float32, jnp.bfloat16


def split3(x):
    hi = x.astype(BF16)
    rest = x - hi.astype(F32)
    mid = rest.astype(BF16)
    low = (rest - mid.astype(F32)).astype(BF16)
    return hi, mid, low


def left6(x):
    h, m, l = split3(x)
    return jnp.concatenate([h, h, m, m, h, l], axis=1)


def right6(x):
    h, m, l = split3(x)
    return jnp.concatenate([h, m, h, m, l, h], axis=0)


def mm(a, b):
    return jnp.dot(left6(a), right6(b), preferred_element_type=F32)


def _transfer_kernel(nbr, steps, det, disp, basis, first, bg, out, rowp, colp, co, w0, w1, bc, pr, mixed, bgp, acc):
    g = pl.program_id(0)
    last = pl.num_programs(0) - 1
    vecs, cycles, samples = bc.shape[2], bc.shape[1], bc.shape[3]
    parts = cycles // UNROLL
    later = jnp.minimum(g + 1, last)

    def turn(left, x):
        return lax.dot_general(left, x, (((1,), (1,)), ((), ())), preferred_element_type=F32)

    def mix_columns(src, ii):
      for i in (2 * ii, 2 * ii + 1):
        cols = pl.ds(pl.multiple_of(i * 256, 256), 256)
        dest = pl.ds(pl.multiple_of(i * 32, 32), 32)
        for p in range(2):
            for h in range(2):
                y = turn(colp[...], src[:, p, h * 16:(h + 1) * 16, cols].reshape(256, 256))
                mixed[p, h, :, dest, :] = y.astype(BF16).reshape(8, 32, 256)

    def swap_rows(ii, group):
      for i in (2 * ii, 2 * ii + 1):
        cols = pl.ds(pl.multiple_of(i * 256, 256), 256)
        dest = pl.ds(pl.multiple_of(group * GROUP, GROUP), GROUP)
        for p in range(2):
            for h in range(2):
                y = turn(rowp[...], mixed[p, h, pl.ds(2 * i, 2)].reshape(256, 256)).reshape(16, 16, 256)
                w0[p, h * 16:(h + 1) * 16, :, cols] = y
                bc[p, h * 16:(h + 1) * 16, dest, cols] = y.astype(BF16)

    @pl.when(g == 0)
    def _():
        i = lax.broadcasted_iota(jnp.int32, (256, 256), 0)
        j = lax.broadcasted_iota(jnp.int32, (256, 256), 1)
        hit = jnp.logical_and(i // 16 == j % 16, i % 16 == j // 16)
        rowp[...] = jnp.where(hit, 1.0, 0.0).astype(BF16)
        hit = j == 8 * (i % 32) + i // 32
        colp[...] = jnp.where(hit, 1.0, 0.0).astype(BF16)

        lines = bg.shape[0] * 2 * cycles
        for n in range(samples // 256):
            terms = split3(bg[:, :, :, n * 256:(n + 1) * 256].reshape(lines, 256))
            for k in range(3):
                y = turn(colp[...], terms[k])
                mixed[k // 2, k % 2, :, n * 32:(n + 1) * 32, 0:lines] = y.astype(BF16).reshape(8, 32, lines)
        i = lax.broadcasted_iota(jnp.int32, (lines, 3 * lines), 0)
        j = lax.broadcasted_iota(jnp.int32, (lines, 3 * lines), 1)
        same = jnp.where(i == j % lines, 1.0, 0.0).astype(BF16)
        for n in range(samples // 128):
            x = jnp.concatenate([mixed[k // 2, k % 2, n, :, 0:lines] for k in range(3)], axis=1)
            bgp[:, :, :, n * 128:(n + 1) * 128] = turn(same, x).reshape(2, 2, cycles, 128)

        @pl.loop(0, cycles)
        def _(r):
            for t in range(2):
                a = bgp[t, 0, pl.ds(r, 1), :]
                b = bgp[t, 1, pl.ds(r, 1), :]
                inten = 2.0 * (a * a + b * b)
                p = a * a - b * b
                q = 2.0 * a * b
                lin = (det[r] + 2.0 * disp[r]) - inten
                for k, val in enumerate((9.0 - q, lin + p, 9.0 + q, p - lin)):
                    co[t, k, r] = jnp.broadcast_to(val, (8, samples))

        @pl.loop(0, parts)
        def _(i):
            mix_columns(first, i)

        @pl.loop(0, parts)
        def _(i):
            swap_rows(i, 0)

    def around(x):
        col = [x[:, 128 * k:128 * k + 128] for k in range(8)]
        col = [pltpu.roll(col[7], 1, 1)] + col + [pltpu.roll(col[0], 127, 1)]
        return jnp.concatenate([col[k] + col[k + 2] for k in range(8)], axis=1)

    def advance(src, t, r):
        n0, n1 = nbr[0, r], nbr[1, r]
        beta = disp[r]
        halves = [slice(lo, lo + 8) for lo in range(0, GROUP, 8)]
        us = [src[0, r, vs, :] for vs in halves]
        vs_ = [src[1, r, vs, :] for vs in halves]
        au = [around(x) for x in us]
        av = [around(x) for x in vs_]
        res = ([[], []], [[], []])
        for k in range(samples // 128):
            lane = slice(128 * k, 128 * k + 128)
            c0, c1, c2, c3 = (co[t, m, r, :, lane] for m in range(4))
            for h, vs in enumerate(halves):
                u, v = us[h][:, lane], vs_[h][:, lane]
                cu = src[0, n0, vs, lane] + src[0, n1, vs, lane]
                cv = src[1, n0, vs, lane] + src[1, n1, vs, lane]
                res[0][h].append((c0 * u + c1 * v) - (beta * av[h][:, lane] + cv))
                res[1][h].append((c2 * v + c3 * u) + (beta * au[h][:, lane] + cu))
        return [[jnp.concatenate(x, axis=1) for x in p] for p in res]

    @pl.loop(0, parts)
    def _(i):
        mix_columns(basis, i)
        for r in [i * UNROLL + k for k in range(UNROLL)]:
            new = advance(w0, 0, r)
            for p in range(2):
                for h in range(2):
                    w1[p, r, 8 * h:8 * h + 8, :] = new[p][h]

    rows = pl.ds(pl.multiple_of(g * GROUP, GROUP), GROUP)

    @pl.when(steps[0] >= 2)
    def _():
        @pl.loop(0, parts)
        def _(i):
            swap_rows(i, later)
            for r in [i * UNROLL + k for k in range(UNROLL)]:
                new = advance(w1, 1, r)
                for p in range(2):
                    full = jnp.concatenate([0.01 * x for x in new[p]], axis=0)
                    pr[p, r, rows, :] = full.astype(BF16)

    @pl.when(steps[0] < 2)
    def _():
        @pl.loop(0, parts)
        def _(i):
            swap_rows(i, later)
            for r in [i * UNROLL + k for k in range(UNROLL)]:
                for p in range(2):
                    pr[p, r, rows, :] = (0.1 * w1[p, r]).astype(BF16)

    @pl.when(g == last)
    def _():
        acc[...] = jnp.zeros_like(acc)

        @pl.loop(0, parts)
        def _(i):
            tot = acc[...]
            for k in range(UNROLL):
                for p in range(2):
                    tot += lax.dot_general(bc[p, i * UNROLL + k], pr[p, i * UNROLL + k], (((1,), (1,)), ((), ())),
                                           preferred_element_type=F32)
            acc[...] = tot

        proj = acc[...]
        gen = 0.25 * (proj - proj.T)
        i = lax.broadcasted_iota(jnp.int32, (vecs, vecs), 0)
        j = lax.broadcasted_iota(jnp.int32, (vecs, vecs), 1)
        eye = jnp.where(i == j, 1.0, 0.0)
        gram = -mm(gen, gen)
        bound = jnp.max(jnp.sum(jnp.abs(gram), axis=0))
        scale = 2.0 / (2.0 + bound)
        resid = eye - scale * (eye + gram)
        prod = scale * (eye + 2.0 * gen - gram)

        def more(c):
            return c[0] > 1e-7

        def body(c):
            rho, rs, pd = c
            return rho * rho, mm(rs, rs), pd + mm(rs, pd)

        out[...] = lax.while_loop(more, body, (0.5 * bound * scale, resid, prod))[2]


def segment_transfer(basis, bg, det, disp, nbr, steps):
    vecs, _, cycles, samples = basis.shape
    smem = pl.BlockSpec(memory_space=pltpu.SMEM)
    groups = vecs // GROUP
    block = (GROUP, 2, cycles, samples)
    return pl.pallas_call(
        _transfer_kernel,
        grid=(groups,),
        out_shape=jax.ShapeDtypeStruct((vecs, vecs), F32),
        in_specs=[smem, smem, smem, smem,
                  pl.BlockSpec(block, lambda g: (jnp.minimum(g + 1, groups - 1), 0, 0, 0)),
                  pl.BlockSpec(block, lambda g: (0, 0, 0, 0), pipeline_mode=pl.Buffered(1)),
                  pl.BlockSpec(bg.shape, lambda g: (0, 0, 0, 0), pipeline_mode=pl.Buffered(1))],
        out_specs=pl.BlockSpec((vecs, vecs), lambda g: (0, 0)),
        scratch_shapes=[
            pltpu.VMEM((256, 256), BF16),
            pltpu.VMEM((256, 256), BF16),
            pltpu.VMEM((2, 4, cycles, 8, samples), F32),
            pltpu.VMEM((2, cycles, GROUP, samples), F32),
            pltpu.VMEM((2, cycles, GROUP, samples), F32),
            pltpu.VMEM((2, cycles, vecs, samples), BF16),
            pltpu.VMEM((2, cycles, vecs, samples), BF16),
            pltpu.VMEM((2, 2, 8, 128, 256), BF16),
            pltpu.VMEM(bg.shape, F32),
            pltpu.VMEM((vecs, vecs), F32),
        ],
        compiler_params=pltpu.CompilerParams(vmem_limit_bytes=63 * 1024 * 1024),
        name="segment_transfer",
    )(nbr.T, steps, det, disp, basis, basis, bg)


def split2(x):
    hi = x.astype(jnp.bfloat16)
    return hi, (x - hi.astype(jnp.float32)).astype(jnp.bfloat16)


def mm3(a, b):
    ah, al = split2(a)
    bh, bl = split2(b)
    return jnp.dot(jnp.concatenate([ah, ah, al], axis=1), jnp.concatenate([bh, bl, bh], axis=0),
                   preferred_element_type=jnp.float32)


def _chain_kernel(t_ref, pre_ref, mono_ref, slots, pair, low, before, send_sem, recv_sem):
    seq, grp = lax.axis_index("seq"), lax.axis_index("grp")
    core = lax.rem(grp, 2)
    depth = lax.rem(lax.div(grp, 2), 4)
    wide = lax.div(grp, 8)
    rounds = (
        (4, seq, lambda pos: (pos, grp)),
        (2, core, lambda pos: (seq, grp - core + pos)),
        (4, depth, lambda pos: (seq, grp + (pos - depth) * 2)),
        (4, wide, lambda pos: (seq, grp + (pos - wide) * 8)),
    )
    mesh_id = pl.DeviceIdType.MESH
    barrier = pltpu.get_barrier_semaphore()
    for radix, pos, place in rounds:
        for hop in range(1, radix):
            pl.semaphore_signal(barrier, inc=1, device_id=place(lax.rem(pos + hop, radix)), device_id_type=mesh_id)
    pl.semaphore_wait(barrier, sum(r[0] - 1 for r in rounds))

    def prefix_step(k, last):
        radix, pos, _ = rounds[k]

        @pl.when(pos == 1)
        def _():
            before[...] = slots[k, 0] if k == 0 else mm3(before[...], slots[k, 0])

        if radix == 4:
            @pl.when(pos == 2)
            def _():
                before[...] = low[...] if k == 0 else mm3(before[...], low[...])

            @pl.when(pos == 3)
            def _():
                left = slots[k, 2] if k == 0 else mm3(before[...], slots[k, 2])
                before[...] = mm3(left, low[...])

    n = t_ref.shape[0]
    i = lax.broadcasted_iota(jnp.int32, (n, n), 0)
    j = lax.broadcasted_iota(jnp.int32, (n, n), 1)
    before[...] = jnp.where(i == j, 1.0, 0.0)
    sends = []
    own = t_ref
    for k, (radix, pos, place) in enumerate(rounds):
        copies = []
        for hop in ((2, 1, 3) if radix == 4 else (1,)):
            copy = pltpu.make_async_remote_copy(
                src_ref=own, dst_ref=slots.at[k, pos], send_sem=send_sem.at[k, hop], recv_sem=recv_sem.at[k, hop],
                device_id=place(lax.rem(pos + hop, radix)), device_id_type=mesh_id)
            copy.start()
            copies.append(copy)
        sends += copies
        slots[k, pos] = own[...]
        if k:
            prefix_step(k - 1, False)
        for copy in copies:
            copy.wait_recv()
        if radix == 4:
            first = mm3(slots[k, 1], slots[k, 0])
            low[...] = first
            total = mm3(mm3(slots[k, 3], slots[k, 2]), first)
        else:
            total = mm3(slots[k, 1], slots[k, 0])
        if k + 1 < len(rounds):
            pair[k] = total
            own = pair.at[k]
        else:
            mono_ref[...] = total
    prefix_step(len(rounds) - 1, True)
    pre_ref[...] = before[...]
    for copy in sends:
        copy.wait_send()


def chain(t):
    n = t.shape[0]
    shape = jax.ShapeDtypeStruct((n, n), jnp.float32)
    vm = pl.BlockSpec(memory_space=pltpu.VMEM)
    return pl.pallas_call(
        _chain_kernel, out_shape=(shape, shape), in_specs=[vm], out_specs=(vm, vm),
        scratch_shapes=[pltpu.VMEM((4, 4, n, n), jnp.float32), pltpu.VMEM((3, n, n), jnp.float32),
                        pltpu.VMEM((n, n), jnp.float32), pltpu.VMEM((n, n), jnp.float32),
                        pltpu.SemaphoreType.DMA((4, 4)), pltpu.SemaphoreType.DMA((4, 4))],
        compiler_params=pltpu.CompilerParams(collective_id=0, has_side_effects=True),
        name="chain_products")(t)

def shards(basis, background, detuning, dispersion, neighbors, step_counts):
    own = segment_transfer(
        basis, background[0, 0], detuning, dispersion, neighbors, step_counts.reshape(1)
    )
    prefix, monodromy = chain(own)
    return (prefix[None, None], monodromy)


def solution(mesh):
    in_specs = (P(), P("grp", "seq", None, None, None, None), P(), P(), P(), P("grp", "seq"))
    out_specs = (P("grp", "seq", None, None), P())
    return jax.shard_map(shards, mesh=mesh, in_specs=in_specs, out_specs=out_specs, check_vma=False)
```

```python
import functools
import jax
import jax.numpy as jnp
from jax import lax
from jax.experimental import pallas as pl
from jax.experimental.pallas import tpu as pltpu
from jax.sharding import PartitionSpec as P

GROUP = 16
UNROLL = 32
F32, BF16 = jnp.float32, jnp.bfloat16


def split3(x):
    hi = x.astype(BF16)
    rest = x - hi.astype(F32)
    mid = rest.astype(BF16)
    low = (rest - mid.astype(F32)).astype(BF16)
    return hi, mid, low


def left6(x):
    h, m, l = split3(x)
    return jnp.concatenate([h, h, m, m, h, l], axis=1)


def right6(x):
    h, m, l = split3(x)
    return jnp.concatenate([h, m, h, m, l, h], axis=0)


def mm(a, b):
    return jnp.dot(left6(a), right6(b), preferred_element_type=F32)


def _transfer_kernel(nbr, steps, det, disp, basis, first, bg, out, rowp, colp, co, w0, w1, bc, pr, mixed, bgp, acc):
    g = pl.program_id(0)
    last = pl.num_programs(0) - 1
    vecs, cycles, samples = bc.shape[2], bc.shape[1], bc.shape[3]
    parts = cycles // UNROLL
    later = jnp.minimum(g + 1, last)

    def turn(left, x):
        return lax.dot_general(left, x, (((1,), (1,)), ((), ())), preferred_element_type=F32)

    def mix_tile(src, k):
        p, h, n = k // 8, k // 4 % 2, k % 4
        y = turn(colp[...], src[:, p, h * 16:(h + 1) * 16, n * 256:(n + 1) * 256].reshape(256, 256))
        mixed[p, h, :, n * 32:(n + 1) * 32, :] = y.astype(BF16).reshape(8, 32, 256)

    def swap_tile(group, k):
        p, h, n = k // 8, k // 4 % 2, k % 4
        dest = pl.ds(pl.multiple_of(group * GROUP, GROUP), GROUP)
        cols = slice(n * 256, (n + 1) * 256)
        y = turn(rowp[...], mixed[p, h, 2 * n:2 * n + 2].reshape(256, 256)).reshape(16, 16, 256)
        w0[p, h * 16:(h + 1) * 16, :, cols] = y
        bc[p, h * 16:(h + 1) * 16, dest, cols] = y.astype(BF16)

    @pl.when(g == 0)
    def _():
        i = lax.broadcasted_iota(jnp.int32, (256, 256), 0)
        j = lax.broadcasted_iota(jnp.int32, (256, 256), 1)
        hit = jnp.logical_and(i // 16 == j % 16, i % 16 == j // 16)
        rowp[...] = jnp.where(hit, 1.0, 0.0).astype(BF16)
        hit = j == 8 * (i % 32) + i // 32
        colp[...] = jnp.where(hit, 1.0, 0.0).astype(BF16)

        lines = bg.shape[0] * 2 * cycles
        for n in range(samples // 256):
            terms = split3(bg[:, :, :, n * 256:(n + 1) * 256].reshape(lines, 256))
            for k in range(3):
                y = turn(colp[...], terms[k])
                mixed[k // 2, k % 2, :, n * 32:(n + 1) * 32, 0:lines] = y.astype(BF16).reshape(8, 32, lines)
        i = lax.broadcasted_iota(jnp.int32, (lines, 3 * lines), 0)
        j = lax.broadcasted_iota(jnp.int32, (lines, 3 * lines), 1)
        same = jnp.where(i == j % lines, 1.0, 0.0).astype(BF16)
        for n in range(samples // 128):
            x = jnp.concatenate([mixed[k // 2, k % 2, n, :, 0:lines] for k in range(3)], axis=1)
            bgp[:, :, :, n * 128:(n + 1) * 128] = turn(same, x).reshape(2, 2, cycles, 128)

        @pl.loop(0, cycles // 4)
        def _(q):
          for r, t in [(4 * q + k, t) for k in range(4) for t in range(2)]:
                a = bgp[t, 0, pl.ds(r, 1), :]
                b = bgp[t, 1, pl.ds(r, 1), :]
                inten = 2.0 * (a * a + b * b)
                p = a * a - b * b
                ab = 2.0 * a * b
                lin = (det[r] + 2.0 * disp[r]) - inten
                for k, val in enumerate((9.0 - ab, lin + p, 9.0 + ab, p - lin)):
                    co[t, k, r] = jnp.broadcast_to(val, (8, samples))

        for k in range(16):
            mix_tile(first, k)
        for k in range(16):
            swap_tile(0, k)

    def around(x):
        col = [x[:, 128 * k:128 * k + 128] for k in range(8)]
        col = [pltpu.roll(col[7], 1, 1)] + col + [pltpu.roll(col[0], 127, 1)]
        return jnp.concatenate([col[k] + col[k + 2] for k in range(8)], axis=1)

    def advance(src, t, r):
        n0, n1 = nbr[0, r], nbr[1, r]
        beta = disp[r]
        halves = [slice(lo, lo + 8) for lo in range(0, GROUP, 8)]
        us = [src[0, r, vs, :] for vs in halves]
        vs_ = [src[1, r, vs, :] for vs in halves]
        au = [around(x) for x in us]
        av = [around(x) for x in vs_]
        res = ([[], []], [[], []])
        for k in range(samples // 128):
            lane = slice(128 * k, 128 * k + 128)
            c0, c1, c2, c3 = (co[t, m, r, :, lane] for m in range(4))
            for h, vs in enumerate(halves):
                u, v = us[h][:, lane], vs_[h][:, lane]
                cu = src[0, n0, vs, lane] + src[0, n1, vs, lane]
                cv = src[1, n0, vs, lane] + src[1, n1, vs, lane]
                res[0][h].append((c0 * u + c1 * v) - (beta * av[h][:, lane] + cv))
                res[1][h].append((c2 * v + c3 * u) + (beta * au[h][:, lane] + cu))
        return [[jnp.concatenate(x, axis=1) for x in p] for p in res]

    for r in range(cycles):
        new = advance(w0, 0, r)
        if r % 2 == 0:
            mix_tile(basis, r // 2)
        for p in range(2):
            for h in range(2):
                w1[p, r, 8 * h:8 * h + 8, :] = new[p][h]

    rows = pl.ds(pl.multiple_of(g * GROUP, GROUP), GROUP)

    @pl.when(steps[0] >= 2)
    def _():
        for r in range(cycles):
            if r % 2 == 0:
                swap_tile(later, r // 2)
            new = advance(w1, 1, r)
            for p in range(2):
                full = jnp.concatenate([0.01 * x for x in new[p]], axis=0)
                pr[p, r, rows, :] = full.astype(BF16)

    @pl.when(steps[0] < 2)
    def _():
        for r in range(cycles):
            if r % 2 == 0:
                swap_tile(later, r // 2)
            for p in range(2):
                pr[p, r, rows, :] = (0.1 * w1[p, r]).astype(BF16)

    @pl.when(g == last)
    def _():
        acc[...] = jnp.zeros_like(acc)

        @pl.loop(0, parts)
        def _(i):
            tot = acc[...]
            for k in range(UNROLL):
                for p in range(2):
                    tot += lax.dot_general(bc[p, i * UNROLL + k], pr[p, i * UNROLL + k], (((1,), (1,)), ((), ())),
                                           preferred_element_type=F32)
            acc[...] = tot

        proj = acc[...]
        gen = 0.25 * (proj - proj.T)
        i = lax.broadcasted_iota(jnp.int32, (vecs, vecs), 0)
        j = lax.broadcasted_iota(jnp.int32, (vecs, vecs), 1)
        eye = jnp.where(i == j, 1.0, 0.0)
        gram = -mm(gen, gen)
        bound = jnp.max(jnp.sum(jnp.abs(gram), axis=0))
        scale = 2.0 / (2.0 + bound)
        resid = eye - scale * (eye + gram)
        prod = scale * (eye + 2.0 * gen - gram)

        def more(c):
            return c[0] > 1e-7

        def body(c):
            rho, rs, pd = c
            return rho * rho, mm(rs, rs), pd + mm(rs, pd)

        out[...] = lax.while_loop(more, body, (0.5 * bound * scale, resid, prod))[2]


def segment_transfer(basis, bg, det, disp, nbr, steps):
    vecs, _, cycles, samples = basis.shape
    smem = pl.BlockSpec(memory_space=pltpu.SMEM)
    groups = vecs // GROUP
    block = (GROUP, 2, cycles, samples)
    return pl.pallas_call(
        _transfer_kernel,
        grid=(groups,),
        out_shape=jax.ShapeDtypeStruct((vecs, vecs), F32),
        in_specs=[smem, smem, smem, smem,
                  pl.BlockSpec(block, lambda g: (jnp.minimum(g + 1, groups - 1), 0, 0, 0)),
                  pl.BlockSpec(block, lambda g: (0, 0, 0, 0), pipeline_mode=pl.Buffered(1)),
                  pl.BlockSpec(bg.shape, lambda g: (0, 0, 0, 0), pipeline_mode=pl.Buffered(1))],
        out_specs=pl.BlockSpec((vecs, vecs), lambda g: (0, 0)),
        scratch_shapes=[
            pltpu.VMEM((256, 256), BF16),
            pltpu.VMEM((256, 256), BF16),
            pltpu.VMEM((2, 4, cycles, 8, samples), F32),
            pltpu.VMEM((2, cycles, GROUP, samples), F32),
            pltpu.VMEM((2, cycles, GROUP, samples), F32),
            pltpu.VMEM((2, cycles, vecs, samples), BF16),
            pltpu.VMEM((2, cycles, vecs, samples), BF16),
            pltpu.VMEM((2, 2, 8, 128, 256), BF16),
            pltpu.VMEM(bg.shape, F32),
            pltpu.VMEM((vecs, vecs), F32),
        ],
        compiler_params=pltpu.CompilerParams(vmem_limit_bytes=63 * 1024 * 1024),
        name="segment_transfer",
    )(nbr.T, steps, det, disp, basis, basis, bg)


def split2(x):
    hi = x.astype(jnp.bfloat16)
    return hi, (x - hi.astype(jnp.float32)).astype(jnp.bfloat16)


def mm3(a, b):
    ah, al = split2(a)
    bh, bl = split2(b)
    return jnp.dot(jnp.concatenate([ah, ah, al], axis=1), jnp.concatenate([bh, bl, bh], axis=0),
                   preferred_element_type=jnp.float32)


def _chain_kernel(t_ref, ends, slots, pair, low, before, send_sem, recv_sem):
    seq, grp = lax.axis_index("seq"), lax.axis_index("grp")
    core = lax.rem(grp, 2)
    depth = lax.rem(lax.div(grp, 2), 4)
    wide = lax.div(grp, 8)
    rounds = (
        (4, seq, lambda pos: (pos, grp)),
        (2, core, lambda pos: (seq, grp - core + pos)),
        (4, depth, lambda pos: (seq, grp + (pos - depth) * 2)),
        (4, wide, lambda pos: (seq, grp + (pos - wide) * 8)),
    )
    mesh_id = pl.DeviceIdType.MESH
    barrier = pltpu.get_barrier_semaphore()
    for radix, pos, place in rounds:
        for hop in range(1, radix):
            pl.semaphore_signal(barrier, inc=1, device_id=place(lax.rem(pos + hop, radix)), device_id_type=mesh_id)
    pl.semaphore_wait(barrier, sum(r[0] - 1 for r in rounds))

    def prefix_step(k):
        radix, pos, _ = rounds[k]

        @pl.when(pos == 1)
        def _():
            before[...] = slots[k, 0] if k == 0 else mm3(before[...], slots[k, 0])

        if radix == 4:
            @pl.when(pos == 2)
            def _():
                before[...] = low[...] if k == 0 else mm3(before[...], low[...])

            @pl.when(pos == 3)
            def _():
                left = slots[k, 2] if k == 0 else mm3(before[...], slots[k, 2])
                before[...] = mm3(left, low[...])

    n = t_ref.shape[0]
    i = lax.broadcasted_iota(jnp.int32, (n, n), 0)
    j = lax.broadcasted_iota(jnp.int32, (n, n), 1)
    eye = jnp.where(i == j, 1.0, 0.0)
    before[...] = eye
    sends = []
    own = t_ref
    for k, (radix, pos, place) in enumerate(rounds):
        copies = []
        for hop in ((2, 1, 3) if radix == 4 else (1,)):
            copy = pltpu.make_async_remote_copy(
                src_ref=own, dst_ref=slots.at[k, pos], send_sem=send_sem.at[k, hop], recv_sem=recv_sem.at[k, hop],
                device_id=place(lax.rem(pos + hop, radix)), device_id_type=mesh_id)
            copy.start()
            copies.append(copy)
        sends += copies
        slots[k, pos] = own[...]
        if k:
            prefix_step(k - 1)
        for copy in copies:
            copy.wait_recv()
        if k + 1 == len(rounds):
            break
        total = mm3(slots[k, 1], slots[k, 0])
        if radix == 4:
            low[...] = total
            total = mm3(mm3(slots[k, 3], slots[k, 2]), total)
        pair[k] = total
        own = pair.at[k]

    k = len(rounds) - 1
    first = mm3(slots[k, 1], slots[k, 0])
    ends[0] = mm3(slots[k, 3], slots[k, 2])
    ends[1] = first
    ends[2] = before[...]
    ends[3] = first

    @pl.when(wide == 3)
    def _():
        ends[2] = mm3(before[...], slots[k, 2])

    @pl.when(wide == 1)
    def _():
        ends[3] = slots[k, 0]

    @pl.when(wide == 0)
    def _():
        ends[3] = eye

    for copy in sends:
        copy.wait_send()


def _finish_kernel(ends, pre_ref, mono_ref):
    mono_ref[...] = mm3(ends[0], ends[1])
    pre_ref[...] = mm3(ends[2], ends[3])


def chain(t):
    n = t.shape[0]
    shape = jax.ShapeDtypeStruct((n, n), jnp.float32)
    vm = pl.BlockSpec(memory_space=pltpu.VMEM)
    ends = pl.pallas_call(
        _chain_kernel, out_shape=jax.ShapeDtypeStruct((4, n, n), jnp.float32), in_specs=[vm], out_specs=vm,
        scratch_shapes=[pltpu.VMEM((4, 4, n, n), jnp.float32), pltpu.VMEM((3, n, n), jnp.float32),
                        pltpu.VMEM((n, n), jnp.float32), pltpu.VMEM((n, n), jnp.float32),
                        pltpu.SemaphoreType.DMA((4, 4)), pltpu.SemaphoreType.DMA((4, 4))],
        compiler_params=pltpu.CompilerParams(collective_id=0, has_side_effects=True),
        name="chain_products")(t)
    return pl.pallas_call(
        _finish_kernel, out_shape=(shape, shape), in_specs=[vm], out_specs=(vm, vm),
        name="last_products")(ends)

def shards(basis, background, detuning, dispersion, neighbors, step_counts):
    own = segment_transfer(
        basis, background[0, 0], detuning, dispersion, neighbors, step_counts.reshape(1)
    )
    prefix, monodromy = chain(own)
    return (prefix[None, None], monodromy)


def solution(mesh):
    in_specs = (P(), P("grp", "seq", None, None, None, None), P(), P(), P(), P("grp", "seq"))
    out_specs = (P("grp", "seq", None, None), P())
    return jax.shard_map(shards, mesh=mesh, in_specs=in_specs, out_specs=out_specs, check_vma=False)
```

```python
import functools
import jax
import jax.numpy as jnp
from jax import lax
from jax.experimental import pallas as pl
from jax.experimental.pallas import tpu as pltpu
from jax.sharding import PartitionSpec as P

GROUP = 16
UNROLL = 32
F32, BF16 = jnp.float32, jnp.bfloat16


def split3(x):
    hi = x.astype(BF16)
    rest = x - hi.astype(F32)
    mid = rest.astype(BF16)
    low = (rest - mid.astype(F32)).astype(BF16)
    return hi, mid, low


def left6(x):
    h, m, l = split3(x)
    return jnp.concatenate([h, h, m, m, h, l], axis=1)


def right6(x):
    h, m, l = split3(x)
    return jnp.concatenate([h, m, h, m, l, h], axis=0)


def mm(a, b):
    return jnp.dot(left6(a), right6(b), preferred_element_type=F32)


def _transfer_kernel(nbr, steps, det, disp, basis, bg, out, rowp, colp, co, w0, w1, bc, pr, mixed, bgp, acc, stage, sems):
    g = pl.program_id(0)
    last = pl.num_programs(0) - 1
    vecs, cycles, samples = bc.shape[2], bc.shape[1], bc.shape[3]
    parts = cycles // UNROLL
    later = g + 1
    slot = lax.rem(later, 2)

    def fetch(block, where):
        return pltpu.make_async_copy(basis.at[pl.ds(block * GROUP, GROUP)], stage.at[where], sems.at[where])

    def turn(left, x):
        return lax.dot_general(left, x, (((1,), (1,)), ((), ())), preferred_element_type=F32)

    def mix_tile(where, k):
        p, h, n = k // 8, k // 4 % 2, k % 4
        y = turn(colp[...], stage[where, :, p, h * 16:(h + 1) * 16, n * 256:(n + 1) * 256].reshape(256, 256))
        mixed[p, h, :, n * 32:(n + 1) * 32, :] = y.astype(BF16).reshape(8, 32, 256)

    def swap_tile(group, k):
        p, h, n = k // 8, k // 4 % 2, k % 4
        dest = pl.ds(pl.multiple_of(group * GROUP, GROUP), GROUP)
        cols = slice(n * 256, (n + 1) * 256)
        y = turn(rowp[...], mixed[p, h, 2 * n:2 * n + 2].reshape(256, 256)).reshape(16, 16, 256)
        w0[p, h * 16:(h + 1) * 16, :, cols] = y
        bc[p, h * 16:(h + 1) * 16, dest, cols] = y.astype(BF16)

    @pl.when(g == 0)
    def _():
        fetch(0, 0).start()
        fetch(1, 1).start()
        i = lax.broadcasted_iota(jnp.int32, (256, 256), 0)
        j = lax.broadcasted_iota(jnp.int32, (256, 256), 1)
        hit = jnp.logical_and(i // 16 == j % 16, i % 16 == j // 16)
        rowp[...] = jnp.where(hit, 1.0, 0.0).astype(BF16)
        hit = j == 8 * (i % 32) + i // 32
        colp[...] = jnp.where(hit, 1.0, 0.0).astype(BF16)

        lines = bg.shape[0] * 2 * cycles
        for n in range(samples // 256):
            terms = split3(bg[:, :, :, n * 256:(n + 1) * 256].reshape(lines, 256))
            for k in range(3):
                y = turn(colp[...], terms[k])
                mixed[k // 2, k % 2, :, n * 32:(n + 1) * 32, 0:lines] = y.astype(BF16).reshape(8, 32, lines)
        i = lax.broadcasted_iota(jnp.int32, (lines, 3 * lines), 0)
        j = lax.broadcasted_iota(jnp.int32, (lines, 3 * lines), 1)
        same = jnp.where(i == j % lines, 1.0, 0.0).astype(BF16)
        for n in range(samples // 128):
            x = jnp.concatenate([mixed[k // 2, k % 2, n, :, 0:lines] for k in range(3)], axis=1)
            bgp[:, :, :, n * 128:(n + 1) * 128] = turn(same, x).reshape(2, 2, cycles, 128)

        @pl.loop(0, cycles // 4)
        def _(q):
          for r, t in [(4 * q + k, t) for k in range(4) for t in range(2)]:
                a = bgp[t, 0, pl.ds(r, 1), :]
                b = bgp[t, 1, pl.ds(r, 1), :]
                inten = 2.0 * (a * a + b * b)
                p = a * a - b * b
                ab = 2.0 * a * b
                lin = (det[r] + 2.0 * disp[r]) - inten
                for k, val in enumerate((9.0 - ab, lin + p, 9.0 + ab, p - lin)):
                    co[t, k, r] = jnp.broadcast_to(val, (8, samples))

        fetch(0, 0).wait()
        for k in range(16):
            mix_tile(0, k)
        fetch(2, 0).start()
        for k in range(16):
            swap_tile(0, k)

    def around(x):
        col = [x[:, 128 * k:128 * k + 128] for k in range(8)]
        col = [pltpu.roll(col[7], 1, 1)] + col + [pltpu.roll(col[0], 127, 1)]
        return jnp.concatenate([col[k] + col[k + 2] for k in range(8)], axis=1)

    def advance(src, t, r):
        n0, n1 = nbr[0, r], nbr[1, r]
        beta = disp[r]
        halves = [slice(lo, lo + 8) for lo in range(0, GROUP, 8)]
        us = [src[0, r, vs, :] for vs in halves]
        vs_ = [src[1, r, vs, :] for vs in halves]
        au = [around(x) for x in us]
        av = [around(x) for x in vs_]
        res = ([[], []], [[], []])
        for k in range(samples // 128):
            lane = slice(128 * k, 128 * k + 128)
            c0, c1, c2, c3 = (co[t, m, r, :, lane] for m in range(4))
            for h, vs in enumerate(halves):
                u, v = us[h][:, lane], vs_[h][:, lane]
                cu = src[0, n0, vs, lane] + src[0, n1, vs, lane]
                cv = src[1, n0, vs, lane] + src[1, n1, vs, lane]
                res[0][h].append((c0 * u + c1 * v) - (beta * av[h][:, lane] + cv))
                res[1][h].append((c2 * v + c3 * u) + (beta * au[h][:, lane] + cu))
        return [[jnp.concatenate(x, axis=1) for x in p] for p in res]

    rows = pl.ds(pl.multiple_of(g * GROUP, GROUP), GROUP)

    def first_step(more):
        for r in range(cycles):
            new = advance(w0, 0, r)
            if more and r % 2 == 0:
                mix_tile(slot, r // 2)
            for p in range(2):
                for h in range(2):
                    w1[p, r, 8 * h:8 * h + 8, :] = new[p][h]

    def second_step(more):
        for r in range(cycles):
            if more and r % 2 == 0:
                swap_tile(later, r // 2)
            new = advance(w1, 1, r)
            for p in range(2):
                full = jnp.concatenate([0.01 * x for x in new[p]], axis=0)
                pr[p, r, rows, :] = full.astype(BF16)

    def keep_first(more):
        for r in range(cycles):
            if more and r % 2 == 0:
                swap_tile(later, r // 2)
            for p in range(2):
                pr[p, r, rows, :] = (0.1 * w1[p, r]).astype(BF16)

    twice = steps[0] >= 2

    @pl.when(g < last)
    def _():
        fetch(later, slot).wait()
        first_step(True)

        @pl.when(g + 3 <= last)
        def _():
            fetch(g + 3, slot).start()

        pl.when(twice)(functools.partial(second_step, True))
        pl.when(jnp.logical_not(twice))(functools.partial(keep_first, True))

    @pl.when(g == last)
    def _():
        first_step(False)
        pl.when(twice)(functools.partial(second_step, False))
        pl.when(jnp.logical_not(twice))(functools.partial(keep_first, False))

    @pl.when(g == last)
    def _():
        acc[...] = jnp.zeros_like(acc)

        @pl.loop(0, parts)
        def _(i):
            tot = acc[...]
            for k in range(UNROLL):
                for p in range(2):
                    tot += lax.dot_general(bc[p, i * UNROLL + k], pr[p, i * UNROLL + k], (((1,), (1,)), ((), ())),
                                           preferred_element_type=F32)
            acc[...] = tot

        proj = acc[...]
        gen = 0.25 * (proj - proj.T)
        i = lax.broadcasted_iota(jnp.int32, (vecs, vecs), 0)
        j = lax.broadcasted_iota(jnp.int32, (vecs, vecs), 1)
        eye = jnp.where(i == j, 1.0, 0.0)
        gram = -mm(gen, gen)
        bound = jnp.max(jnp.sum(jnp.abs(gram), axis=0))
        scale = 2.0 / (2.0 + bound)
        resid = eye - scale * (eye + gram)
        prod = scale * (eye + 2.0 * gen - gram)

        def more(c):
            return c[0] > 1e-7

        def body(c):
            rho, rs, pd = c
            return rho * rho, mm(rs, rs), pd + mm(rs, pd)

        out[...] = lax.while_loop(more, body, (0.5 * bound * scale, resid, prod))[2]


def segment_transfer(basis, bg, det, disp, nbr, steps):
    vecs, _, cycles, samples = basis.shape
    smem = pl.BlockSpec(memory_space=pltpu.SMEM)
    groups = vecs // GROUP
    block = (GROUP, 2, cycles, samples)
    return pl.pallas_call(
        _transfer_kernel,
        grid=(groups,),
        out_shape=jax.ShapeDtypeStruct((vecs, vecs), F32),
        in_specs=[smem, smem, smem, smem,
                  pl.BlockSpec(memory_space=pl.ANY),
                  pl.BlockSpec(bg.shape, lambda g: (0, 0, 0, 0), pipeline_mode=pl.Buffered(1))],
        out_specs=pl.BlockSpec((vecs, vecs), lambda g: (0, 0)),
        scratch_shapes=[
            pltpu.VMEM((256, 256), BF16),
            pltpu.VMEM((256, 256), BF16),
            pltpu.VMEM((2, 4, cycles, 8, samples), F32),
            pltpu.VMEM((2, cycles, GROUP, samples), F32),
            pltpu.VMEM((2, cycles, GROUP, samples), F32),
            pltpu.VMEM((2, cycles, vecs, samples), BF16),
            pltpu.VMEM((2, cycles, vecs, samples), BF16),
            pltpu.VMEM((2, 2, 8, 128, 256), BF16),
            pltpu.VMEM(bg.shape, F32),
            pltpu.VMEM((vecs, vecs), F32),
            pltpu.VMEM((2,) + block, BF16),
            pltpu.SemaphoreType.DMA((2,)),
        ],
        compiler_params=pltpu.CompilerParams(vmem_limit_bytes=63 * 1024 * 1024),
        name="segment_transfer",
    )(nbr.T, steps, det, disp, basis, bg)


def split2(x):
    hi = x.astype(jnp.bfloat16)
    return hi, (x - hi.astype(jnp.float32)).astype(jnp.bfloat16)


def mm3(a, b):
    ah, al = split2(a)
    bh, bl = split2(b)
    return jnp.dot(jnp.concatenate([ah, ah, al], axis=1), jnp.concatenate([bh, bl, bh], axis=0),
                   preferred_element_type=jnp.float32)


def _chain_kernel(t_ref, ends, slots, pair, low, before, send_sem, recv_sem):
    seq, grp = lax.axis_index("seq"), lax.axis_index("grp")
    core = lax.rem(grp, 2)
    depth = lax.rem(lax.div(grp, 2), 4)
    wide = lax.div(grp, 8)
    rounds = (
        (4, seq, lambda pos: (pos, grp)),
        (2, core, lambda pos: (seq, grp - core + pos)),
        (4, depth, lambda pos: (seq, grp + (pos - depth) * 2)),
        (4, wide, lambda pos: (seq, grp + (pos - wide) * 8)),
    )
    mesh_id = pl.DeviceIdType.MESH
    barrier = pltpu.get_barrier_semaphore()
    for radix, pos, place in rounds:
        for hop in range(1, radix):
            pl.semaphore_signal(barrier, inc=1, device_id=place(lax.rem(pos + hop, radix)), device_id_type=mesh_id)
    pl.semaphore_wait(barrier, sum(r[0] - 1 for r in rounds))

    def prefix_step(k):
        radix, pos, _ = rounds[k]

        @pl.when(pos == 1)
        def _():
            before[...] = slots[k, 0] if k == 0 else mm3(before[...], slots[k, 0])

        if radix == 4:
            @pl.when(pos == 2)
            def _():
                before[...] = low[...] if k == 0 else mm3(before[...], low[...])

            @pl.when(pos == 3)
            def _():
                left = slots[k, 2] if k == 0 else mm3(before[...], slots[k, 2])
                before[...] = mm3(left, low[...])

    n = t_ref.shape[0]
    i = lax.broadcasted_iota(jnp.int32, (n, n), 0)
    j = lax.broadcasted_iota(jnp.int32, (n, n), 1)
    eye = jnp.where(i == j, 1.0, 0.0)
    before[...] = eye
    sends = []
    own = t_ref
    for k, (radix, pos, place) in enumerate(rounds):
        copies = []
        for hop in ((1, 3, 2) if radix == 4 else (1,)):
            copy = pltpu.make_async_remote_copy(
                src_ref=own, dst_ref=slots.at[k, pos], send_sem=send_sem.at[k, hop], recv_sem=recv_sem.at[k, hop],
                device_id=place(lax.rem(pos + hop, radix)), device_id_type=mesh_id)
            copy.start()
            copies.append(copy)
        sends += copies
        slots[k, pos] = own[...]
        if k:
            prefix_step(k - 1)
        for copy in copies:
            copy.wait_recv()
        if k + 1 == len(rounds):
            break
        total = mm3(slots[k, 1], slots[k, 0])
        if radix == 4:
            low[...] = total
            total = mm3(mm3(slots[k, 3], slots[k, 2]), total)
        pair[k] = total
        own = pair.at[k]

    k = len(rounds) - 1
    first = mm3(slots[k, 1], slots[k, 0])
    ends[0] = mm3(slots[k, 3], slots[k, 2])
    ends[1] = first
    ends[2] = before[...]
    ends[3] = first

    @pl.when(wide == 3)
    def _():
        ends[2] = mm3(before[...], slots[k, 2])

    @pl.when(wide == 1)
    def _():
        ends[3] = slots[k, 0]

    @pl.when(wide == 0)
    def _():
        ends[3] = eye

    for copy in sends:
        copy.wait_send()


def _finish_kernel(ends, pre_ref, mono_ref):
    mono_ref[...] = mm3(ends[0], ends[1])
    pre_ref[...] = mm3(ends[2], ends[3])


def chain(t):
    n = t.shape[0]
    shape = jax.ShapeDtypeStruct((n, n), jnp.float32)
    vm = pl.BlockSpec(memory_space=pltpu.VMEM)
    ends = pl.pallas_call(
        _chain_kernel, out_shape=jax.ShapeDtypeStruct((4, n, n), jnp.float32), in_specs=[vm], out_specs=vm,
        scratch_shapes=[pltpu.VMEM((4, 4, n, n), jnp.float32), pltpu.VMEM((3, n, n), jnp.float32),
                        pltpu.VMEM((n, n), jnp.float32), pltpu.VMEM((n, n), jnp.float32),
                        pltpu.SemaphoreType.DMA((4, 4)), pltpu.SemaphoreType.DMA((4, 4))],
        compiler_params=pltpu.CompilerParams(collective_id=0, has_side_effects=True),
        name="chain_products")(t)
    return pl.pallas_call(
        _finish_kernel, out_shape=(shape, shape), in_specs=[vm], out_specs=(vm, vm),
        name="last_products")(ends)

def shards(basis, background, detuning, dispersion, neighbors, step_counts):
    own = segment_transfer(
        basis, background[0, 0], detuning, dispersion, neighbors, step_counts.reshape(1)
    )
    prefix, monodromy = chain(own)
    return (prefix[None, None], monodromy)


def solution(mesh):
    in_specs = (P(), P("grp", "seq", None, None, None, None), P(), P(), P(), P("grp", "seq"))
    out_specs = (P("grp", "seq", None, None), P())
    return jax.shard_map(shards, mesh=mesh, in_specs=in_specs, out_specs=out_specs, check_vma=False)
```

```python
import functools
import jax
import jax.numpy as jnp
from jax import lax
from jax.experimental import pallas as pl
from jax.experimental.pallas import tpu as pltpu
from jax.sharding import PartitionSpec as P

GROUP = 16
UNROLL = 32
F32, BF16 = jnp.float32, jnp.bfloat16


def split3(x):
    hi = x.astype(BF16)
    rest = x - hi.astype(F32)
    mid = rest.astype(BF16)
    low = (rest - mid.astype(F32)).astype(BF16)
    return hi, mid, low


def left6(x):
    h, m, l = split3(x)
    return jnp.concatenate([h, h, m, m, h, l], axis=1)


def right6(x):
    h, m, l = split3(x)
    return jnp.concatenate([h, m, h, m, l, h], axis=0)


def mm(a, b):
    return jnp.dot(left6(a), right6(b), preferred_element_type=F32)


def _transfer_kernel(nbr, steps, det, disp, basis, bg, out, rowp, colp, co, w0, w1, bc, pr, mixed, bgp, acc, stage, sems):
    g = pl.program_id(0)
    last = pl.num_programs(0) - 1
    vecs, cycles, samples = bc.shape[2], bc.shape[1], bc.shape[3]
    parts = cycles // UNROLL
    later = g + 1
    slot = lax.rem(later, 2)

    def fetch(block, where):
        return pltpu.make_async_copy(basis.at[pl.ds(block * GROUP, GROUP)], stage.at[where], sems.at[where])

    def turn(left, x):
        return lax.dot_general(left, x, (((1,), (1,)), ((), ())), preferred_element_type=F32)

    def mix_tile(where, k):
        p, h, n = k // 8, k // 4 % 2, k % 4
        y = turn(colp[...], stage[where, :, p, h * 16:(h + 1) * 16, n * 256:(n + 1) * 256].reshape(256, 256))
        mixed[p, h, :, n * 32:(n + 1) * 32, :] = y.astype(BF16).reshape(8, 32, 256)

    def swap_tile(group, k):
        p, h, n = k // 8, k // 4 % 2, k % 4
        dest = pl.ds(pl.multiple_of(group * GROUP, GROUP), GROUP)
        cols = slice(n * 256, (n + 1) * 256)
        y = turn(rowp[...], mixed[p, h, 2 * n:2 * n + 2].reshape(256, 256)).reshape(16, 16, 256)
        w0[p, h * 16:(h + 1) * 16, :, cols] = y
        bc[p, h * 16:(h + 1) * 16, dest, cols] = y.astype(BF16)

    @pl.when(g == 0)
    def _():
        fetch(0, 0).start()
        fetch(1, 1).start()
        i = lax.broadcasted_iota(jnp.int32, (256, 256), 0)
        j = lax.broadcasted_iota(jnp.int32, (256, 256), 1)
        hit = jnp.logical_and(i // 16 == j % 16, i % 16 == j // 16)
        rowp[...] = jnp.where(hit, 1.0, 0.0).astype(BF16)
        hit = j == 8 * (i % 32) + i // 32
        colp[...] = jnp.where(hit, 1.0, 0.0).astype(BF16)

        lines = bg.shape[0] * 2 * cycles
        for n in range(samples // 256):
            terms = split3(bg[:, :, :, n * 256:(n + 1) * 256].reshape(lines, 256))
            for k in range(3):
                y = turn(colp[...], terms[k])
                mixed[k // 2, k % 2, :, n * 32:(n + 1) * 32, 0:lines] = y.astype(BF16).reshape(8, 32, lines)
        i = lax.broadcasted_iota(jnp.int32, (lines, 3 * lines), 0)
        j = lax.broadcasted_iota(jnp.int32, (lines, 3 * lines), 1)
        same = jnp.where(i == j % lines, 1.0, 0.0).astype(BF16)
        for n in range(samples // 128):
            x = jnp.concatenate([mixed[k // 2, k % 2, n, :, 0:lines] for k in range(3)], axis=1)
            bgp[:, :, :, n * 128:(n + 1) * 128] = turn(same, x).reshape(2, 2, cycles, 128)

        @pl.loop(0, cycles // 4)
        def _(q):
          for r, t in [(4 * q + k, t) for k in range(4) for t in range(2)]:
                a = bgp[t, 0, pl.ds(r, 1), :]
                b = bgp[t, 1, pl.ds(r, 1), :]
                inten = 2.0 * (a * a + b * b)
                p = a * a - b * b
                ab = 2.0 * a * b
                lin = (det[r] + 2.0 * disp[r]) - inten
                for k, val in enumerate((9.0 - ab, lin + p, 9.0 + ab, p - lin)):
                    co[t, k, r] = jnp.broadcast_to(val, (8, samples))

        fetch(0, 0).wait()
        for k in range(16):
            mix_tile(0, k)
        fetch(2, 0).start()
        for k in range(16):
            swap_tile(0, k)

    def around(x):
        col = [x[:, 128 * k:128 * k + 128] for k in range(8)]
        col = [pltpu.roll(col[7], 1, 1)] + col + [pltpu.roll(col[0], 127, 1)]
        return jnp.concatenate([col[k] + col[k + 2] for k in range(8)], axis=1)

    def advance(src, t, r):
        n0, n1 = nbr[0, r], nbr[1, r]
        beta = disp[r]
        halves = [slice(lo, lo + 8) for lo in range(0, GROUP, 8)]
        us = [src[0, r, vs, :] for vs in halves]
        vs_ = [src[1, r, vs, :] for vs in halves]
        au = [around(x) for x in us]
        av = [around(x) for x in vs_]
        res = ([[], []], [[], []])
        for k in range(samples // 128):
            lane = slice(128 * k, 128 * k + 128)
            c0, c1, c2, c3 = (co[t, m, r, :, lane] for m in range(4))
            for h, vs in enumerate(halves):
                u, v = us[h][:, lane], vs_[h][:, lane]
                cu = src[0, n0, vs, lane] + src[0, n1, vs, lane]
                cv = src[1, n0, vs, lane] + src[1, n1, vs, lane]
                res[0][h].append((c0 * u + c1 * v) - (beta * av[h][:, lane] + cv))
                res[1][h].append((c2 * v + c3 * u) + (beta * au[h][:, lane] + cu))
        return [[jnp.concatenate(x, axis=1) for x in p] for p in res]

    rows = pl.ds(pl.multiple_of(g * GROUP, GROUP), GROUP)

    def first_step(more):
        for r in range(cycles):
            new = advance(w0, 0, r)
            if more and r % 2 == 0:
                mix_tile(slot, r // 2)
            for p in range(2):
                for h in range(2):
                    w1[p, r, 8 * h:8 * h + 8, :] = new[p][h]

    def second_step(more):
        for r in range(cycles):
            if more and r % 2 == 0:
                swap_tile(later, r // 2)
            new = advance(w1, 1, r)
            for p in range(2):
                full = jnp.concatenate([0.01 * x for x in new[p]], axis=0)
                pr[p, r, rows, :] = full.astype(BF16)

    def keep_first(more):
        for r in range(cycles):
            if more and r % 2 == 0:
                swap_tile(later, r // 2)
            for p in range(2):
                pr[p, r, rows, :] = (0.1 * w1[p, r]).astype(BF16)

    twice = steps[0] >= 2

    @pl.when(g < last)
    def _():
        fetch(later, slot).wait()
        first_step(True)

        @pl.when(g + 3 <= last)
        def _():
            fetch(g + 3, slot).start()

        pl.when(twice)(functools.partial(second_step, True))
        pl.when(jnp.logical_not(twice))(functools.partial(keep_first, True))

    @pl.when(g == last)
    def _():
        first_step(False)
        pl.when(twice)(functools.partial(second_step, False))
        pl.when(jnp.logical_not(twice))(functools.partial(keep_first, False))

    @pl.when(g == last)
    def _():
        acc[...] = jnp.zeros_like(acc)

        @pl.loop(0, parts)
        def _(i):
            tot = acc[...]
            for k in range(UNROLL):
                for p in range(2):
                    tot += lax.dot_general(bc[p, i * UNROLL + k], pr[p, i * UNROLL + k], (((1,), (1,)), ((), ())),
                                           preferred_element_type=F32)
            acc[...] = tot

        proj = acc[...]
        gen = 0.25 * (proj - proj.T)
        i = lax.broadcasted_iota(jnp.int32, (vecs, vecs), 0)
        j = lax.broadcasted_iota(jnp.int32, (vecs, vecs), 1)
        eye = jnp.where(i == j, 1.0, 0.0)
        gram = -mm(gen, gen)
        bound = jnp.max(jnp.sum(jnp.abs(gram), axis=0))
        scale = 2.0 / (2.0 + bound)
        resid = eye - scale * (eye + gram)
        prod = scale * (eye + 2.0 * gen - gram)

        def more(c):
            return 1.0 - c[0] > 3e-7

        def body(c):
            gap, rs, pd = c
            return gap * (2.0 - gap), mm(rs, rs), pd + mm(rs, pd)

        out[...] = lax.while_loop(more, body, (scale, resid, prod))[2]


def segment_transfer(basis, bg, det, disp, nbr, steps):
    vecs, _, cycles, samples = basis.shape
    smem = pl.BlockSpec(memory_space=pltpu.SMEM)
    groups = vecs // GROUP
    block = (GROUP, 2, cycles, samples)
    return pl.pallas_call(
        _transfer_kernel,
        grid=(groups,),
        out_shape=jax.ShapeDtypeStruct((vecs, vecs), F32),
        in_specs=[smem, smem, smem, smem,
                  pl.BlockSpec(memory_space=pl.ANY),
                  pl.BlockSpec(bg.shape, lambda g: (0, 0, 0, 0), pipeline_mode=pl.Buffered(1))],
        out_specs=pl.BlockSpec((vecs, vecs), lambda g: (0, 0)),
        scratch_shapes=[
            pltpu.VMEM((256, 256), BF16),
            pltpu.VMEM((256, 256), BF16),
            pltpu.VMEM((2, 4, cycles, 8, samples), F32),
            pltpu.VMEM((2, cycles, GROUP, samples), F32),
            pltpu.VMEM((2, cycles, GROUP, samples), F32),
            pltpu.VMEM((2, cycles, vecs, samples), BF16),
            pltpu.VMEM((2, cycles, vecs, samples), BF16),
            pltpu.VMEM((2, 2, 8, 128, 256), BF16),
            pltpu.VMEM(bg.shape, F32),
            pltpu.VMEM((vecs, vecs), F32),
            pltpu.VMEM((2,) + block, BF16),
            pltpu.SemaphoreType.DMA((2,)),
        ],
        compiler_params=pltpu.CompilerParams(vmem_limit_bytes=63 * 1024 * 1024),
        name="segment_transfer",
    )(nbr.T, steps, det, disp, basis, bg)


def split2(x):
    hi = x.astype(jnp.bfloat16)
    return hi, (x - hi.astype(jnp.float32)).astype(jnp.bfloat16)


def mm3(a, b):
    ah, al = split2(a)
    bh, bl = split2(b)
    return jnp.dot(jnp.concatenate([ah, ah, al], axis=1), jnp.concatenate([bh, bl, bh], axis=0),
                   preferred_element_type=jnp.float32)


def _chain_kernel(t_ref, ends, slots, pair, low, before, send_sem, recv_sem):
    seq, grp = lax.axis_index("seq"), lax.axis_index("grp")
    core = lax.rem(grp, 2)
    depth = lax.rem(lax.div(grp, 2), 4)
    wide = lax.div(grp, 8)
    rounds = (
        (4, seq, lambda pos: (pos, grp)),
        (2, core, lambda pos: (seq, grp - core + pos)),
        (4, depth, lambda pos: (seq, grp + (pos - depth) * 2)),
        (4, wide, lambda pos: (seq, grp + (pos - wide) * 8)),
    )
    mesh_id = pl.DeviceIdType.MESH
    barrier = pltpu.get_barrier_semaphore()
    for radix, pos, place in rounds:
        for hop in range(1, radix):
            pl.semaphore_signal(barrier, inc=1, device_id=place(lax.rem(pos + hop, radix)), device_id_type=mesh_id)
    pl.semaphore_wait(barrier, sum(r[0] - 1 for r in rounds))

    def prefix_step(k):
        radix, pos, _ = rounds[k]

        @pl.when(pos == 1)
        def _():
            before[...] = slots[k, 0] if k == 0 else mm3(before[...], slots[k, 0])

        if radix == 4:
            @pl.when(pos == 2)
            def _():
                before[...] = low[...] if k == 0 else mm3(before[...], low[...])

            @pl.when(pos == 3)
            def _():
                left = slots[k, 2] if k == 0 else mm3(before[...], slots[k, 2])
                before[...] = mm3(left, low[...])

    n = t_ref.shape[0]
    i = lax.broadcasted_iota(jnp.int32, (n, n), 0)
    j = lax.broadcasted_iota(jnp.int32, (n, n), 1)
    eye = jnp.where(i == j, 1.0, 0.0)
    before[...] = eye
    sends = []
    own = t_ref
    for k, (radix, pos, place) in enumerate(rounds):
        copies = []
        for hop in ((1, 3, 2) if radix == 4 else (1,)):
            copy = pltpu.make_async_remote_copy(
                src_ref=own, dst_ref=slots.at[k, pos], send_sem=send_sem.at[k, hop], recv_sem=recv_sem.at[k, hop],
                device_id=place(lax.rem(pos + hop, radix)), device_id_type=mesh_id)
            copy.start()
            copies.append(copy)
        sends += copies
        slots[k, pos] = own[...]
        if k:
            prefix_step(k - 1)
        for copy in copies:
            copy.wait_recv()
        if k + 1 == len(rounds):
            break
        total = mm3(slots[k, 1], slots[k, 0])
        if radix == 4:
            low[...] = total
            total = mm3(mm3(slots[k, 3], slots[k, 2]), total)
        pair[k] = total
        own = pair.at[k]

    k = len(rounds) - 1
    first = mm3(slots[k, 1], slots[k, 0])
    ends[0] = mm3(slots[k, 3], slots[k, 2])
    ends[1] = first
    ends[2] = before[...]
    ends[3] = first

    @pl.when(wide == 3)
    def _():
        ends[2] = mm3(before[...], slots[k, 2])

    @pl.when(wide == 1)
    def _():
        ends[3] = slots[k, 0]

    @pl.when(wide == 0)
    def _():
        ends[3] = eye

    for copy in sends:
        copy.wait_send()


def _finish_kernel(ends, pre_ref, mono_ref):
    mono_ref[...] = mm3(ends[0], ends[1])
    pre_ref[...] = mm3(ends[2], ends[3])


def chain(t):
    n = t.shape[0]
    shape = jax.ShapeDtypeStruct((n, n), jnp.float32)
    vm = pl.BlockSpec(memory_space=pltpu.VMEM)
    ends = pl.pallas_call(
        _chain_kernel, out_shape=jax.ShapeDtypeStruct((4, n, n), jnp.float32), in_specs=[vm], out_specs=vm,
        scratch_shapes=[pltpu.VMEM((4, 4, n, n), jnp.float32), pltpu.VMEM((3, n, n), jnp.float32),
                        pltpu.VMEM((n, n), jnp.float32), pltpu.VMEM((n, n), jnp.float32),
                        pltpu.SemaphoreType.DMA((4, 4)), pltpu.SemaphoreType.DMA((4, 4))],
        compiler_params=pltpu.CompilerParams(collective_id=0, has_side_effects=True),
        name="chain_products")(t)
    return pl.pallas_call(
        _finish_kernel, out_shape=(shape, shape), in_specs=[vm], out_specs=(vm, vm),
        name="last_products")(ends)

def shards(basis, background, detuning, dispersion, neighbors, step_counts):
    own = segment_transfer(
        basis, background[0, 0], detuning, dispersion, neighbors, step_counts.reshape(1)
    )
    prefix, monodromy = chain(own)
    return (prefix[None, None], monodromy)


def solution(mesh):
    in_specs = (P(), P("grp", "seq", None, None, None, None), P(), P(), P(), P("grp", "seq"))
    out_specs = (P("grp", "seq", None, None), P())
    return jax.shard_map(shards, mesh=mesh, in_specs=in_specs, out_specs=out_specs, check_vma=False)
```

```python
import functools
import jax
import jax.numpy as jnp
from jax import lax
from jax.experimental import pallas as pl
from jax.experimental.pallas import tpu as pltpu
from jax.sharding import PartitionSpec as P

GROUP = 16
UNROLL = 32
F32, BF16 = jnp.float32, jnp.bfloat16


def split3(x):
    hi = x.astype(BF16)
    rest = x - hi.astype(F32)
    mid = rest.astype(BF16)
    low = (rest - mid.astype(F32)).astype(BF16)
    return hi, mid, low


def left6(x):
    h, m, l = split3(x)
    return jnp.concatenate([h, h, m, m, h, l], axis=1)


def right6(x):
    h, m, l = split3(x)
    return jnp.concatenate([h, m, h, m, l, h], axis=0)


def mm(a, b):
    return jnp.dot(left6(a), right6(b), preferred_element_type=F32)


def _transfer_kernel(nbr, steps, det, disp, basis, bg, out, rowp, colp, co, w0, w1, bc, pr, mixed, bgp, acc, stage, sems):
    g = pl.program_id(0)
    last = pl.num_programs(0) - 1
    vecs, cycles, samples = bc.shape[2], bc.shape[1], bc.shape[3]
    parts = cycles // UNROLL
    later = g + 1
    slot = lax.rem(later, 2)

    def fetch(block, where):
        return pltpu.make_async_copy(basis.at[pl.ds(block * GROUP, GROUP)], stage.at[where], sems.at[where])

    def turn(left, x):
        return lax.dot_general(left, x, (((1,), (1,)), ((), ())), preferred_element_type=F32)

    def mix_tile(where, k):
        p, h, n = k // 8, k // 4 % 2, k % 4
        y = turn(colp[...], stage[where, :, p, h * 16:(h + 1) * 16, n * 256:(n + 1) * 256].reshape(256, 256))
        mixed[p, h, :, n * 32:(n + 1) * 32, :] = y.astype(BF16).reshape(8, 32, 256)

    def swap_tile(group, k):
        p, h, n = k // 8, k // 4 % 2, k % 4
        dest = pl.ds(pl.multiple_of(group * GROUP, GROUP), GROUP)
        cols = slice(n * 256, (n + 1) * 256)
        y = turn(rowp[...], mixed[p, h, 2 * n:2 * n + 2].reshape(256, 256)).reshape(16, 16, 256)
        w0[p, h * 16:(h + 1) * 16, :, cols] = y
        bc[p, h * 16:(h + 1) * 16, dest, cols] = y.astype(BF16)

    @pl.when(g == 0)
    def _():
        fetch(0, 0).start()
        fetch(1, 1).start()
        i = lax.broadcasted_iota(jnp.int32, (256, 256), 0)
        j = lax.broadcasted_iota(jnp.int32, (256, 256), 1)
        hit = jnp.logical_and(i // 16 == j % 16, i % 16 == j // 16)
        rowp[...] = jnp.where(hit, 1.0, 0.0).astype(BF16)
        hit = j == 8 * (i % 32) + i // 32
        colp[...] = jnp.where(hit, 1.0, 0.0).astype(BF16)

        lines = bg.shape[0] * 2 * cycles
        for n in range(samples // 256):
            terms = split3(bg[:, :, :, n * 256:(n + 1) * 256].reshape(lines, 256))
            for k in range(3):
                y = turn(colp[...], terms[k])
                mixed[k // 2, k % 2, :, n * 32:(n + 1) * 32, 0:lines] = y.astype(BF16).reshape(8, 32, lines)
        i = lax.broadcasted_iota(jnp.int32, (lines, 3 * lines), 0)
        j = lax.broadcasted_iota(jnp.int32, (lines, 3 * lines), 1)
        same = jnp.where(i == j % lines, 1.0, 0.0).astype(BF16)
        for n in range(samples // 128):
            x = jnp.concatenate([mixed[k // 2, k % 2, n, :, 0:lines] for k in range(3)], axis=1)
            bgp[:, :, :, n * 128:(n + 1) * 128] = turn(same, x).reshape(2, 2, cycles, 128)

        @pl.loop(0, cycles // 4)
        def _(q):
          for r, t in [(4 * q + k, t) for k in range(4) for t in range(2)]:
                a = bgp[t, 0, pl.ds(r, 1), :]
                b = bgp[t, 1, pl.ds(r, 1), :]
                inten = 2.0 * (a * a + b * b)
                p = a * a - b * b
                ab = 2.0 * a * b
                lin = (det[r] + 2.0 * disp[r]) - inten
                for k, val in enumerate((9.0 - ab, lin + p, 9.0 + ab, p - lin)):
                    co[t, k, r] = jnp.broadcast_to(val, (8, samples))

        fetch(0, 0).wait()
        for k in range(16):
            mix_tile(0, k)
        fetch(2, 0).start()
        for k in range(16):
            swap_tile(0, k)

    def around(x):
        col = [x[:, 128 * k:128 * k + 128] for k in range(8)]
        col = [pltpu.roll(col[7], 1, 1)] + col + [pltpu.roll(col[0], 127, 1)]
        return jnp.concatenate([col[k] + col[k + 2] for k in range(8)], axis=1)

    def advance(src, t, r):
        n0, n1 = nbr[0, r], nbr[1, r]
        beta = disp[r]
        halves = [slice(lo, lo + 8) for lo in range(0, GROUP, 8)]
        us = [src[0, r, vs, :] for vs in halves]
        vs_ = [src[1, r, vs, :] for vs in halves]
        au = [around(x) for x in us]
        av = [around(x) for x in vs_]
        res = ([[], []], [[], []])
        for k in range(samples // 128):
            lane = slice(128 * k, 128 * k + 128)
            c0, c1, c2, c3 = (co[t, m, r, :, lane] for m in range(4))
            for h, vs in enumerate(halves):
                u, v = us[h][:, lane], vs_[h][:, lane]
                cu = src[0, n0, vs, lane] + src[0, n1, vs, lane]
                cv = src[1, n0, vs, lane] + src[1, n1, vs, lane]
                res[0][h].append((c0 * u + c1 * v) - (beta * av[h][:, lane] + cv))
                res[1][h].append((c2 * v + c3 * u) + (beta * au[h][:, lane] + cu))
        return [[jnp.concatenate(x, axis=1) for x in p] for p in res]

    rows = pl.ds(pl.multiple_of(g * GROUP, GROUP), GROUP)

    def first_step(more):
        for r in range(cycles):
            new = advance(w0, 0, r)
            if more and r % 2 == 0:
                mix_tile(slot, r // 2)
            for p in range(2):
                for h in range(2):
                    w1[p, r, 8 * h:8 * h + 8, :] = new[p][h]

    def second_step(more):
        for r in range(cycles):
            if more and r % 2 == 0:
                swap_tile(later, r // 2)
            new = advance(w1, 1, r)
            for p in range(2):
                full = jnp.concatenate([0.01 * x for x in new[p]], axis=0)
                pr[p, r, rows, :] = full.astype(BF16)

    def keep_first(more):
        for r in range(cycles):
            if more and r % 2 == 0:
                swap_tile(later, r // 2)
            for p in range(2):
                pr[p, r, rows, :] = (0.1 * w1[p, r]).astype(BF16)

    twice = steps[0] >= 2

    @pl.when(g < last)
    def _():
        fetch(later, slot).wait()
        first_step(True)

        @pl.when(g + 3 <= last)
        def _():
            fetch(g + 3, slot).start()

        pl.when(twice)(functools.partial(second_step, True))
        pl.when(jnp.logical_not(twice))(functools.partial(keep_first, True))

    @pl.when(g == last)
    def _():
        first_step(False)
        pl.when(twice)(functools.partial(second_step, False))
        pl.when(jnp.logical_not(twice))(functools.partial(keep_first, False))

    @pl.when(g == last)
    def _():
        acc[...] = jnp.zeros_like(acc)

        @pl.loop(0, parts)
        def _(i):
            tot = acc[...]
            for k in range(UNROLL):
                for p in range(2):
                    tot += lax.dot_general(bc[p, i * UNROLL + k], pr[p, i * UNROLL + k], (((1,), (1,)), ((), ())),
                                           preferred_element_type=F32)
            acc[...] = tot

        proj = acc[...]
        gen = 0.25 * (proj - proj.T)
        i = lax.broadcasted_iota(jnp.int32, (vecs, vecs), 0)
        j = lax.broadcasted_iota(jnp.int32, (vecs, vecs), 1)
        eye = jnp.where(i == j, 1.0, 0.0)
        gram = -mm(gen, gen)
        bound = jnp.max(jnp.sum(jnp.abs(gram), axis=0))
        scale = 2.0 / (2.0 + bound)
        resid = eye - scale * (eye + gram)
        prod = scale * (eye + 2.0 * gen - gram)

        def more(c):
            return 1.0 - c[0] > 3e-7

        def body(c):
            gap, rs, pd = c
            both = jnp.dot(left6(rs), jnp.concatenate([right6(rs), right6(pd)], axis=1), preferred_element_type=F32)
            return gap * (2.0 - gap), both[:, :vecs], pd + both[:, vecs:]

        out[...] = lax.while_loop(more, body, (scale, resid, prod))[2]


def segment_transfer(basis, bg, det, disp, nbr, steps):
    vecs, _, cycles, samples = basis.shape
    smem = pl.BlockSpec(memory_space=pltpu.SMEM)
    groups = vecs // GROUP
    block = (GROUP, 2, cycles, samples)
    return pl.pallas_call(
        _transfer_kernel,
        grid=(groups,),
        out_shape=jax.ShapeDtypeStruct((vecs, vecs), F32),
        in_specs=[smem, smem, smem, smem,
                  pl.BlockSpec(memory_space=pl.ANY),
                  pl.BlockSpec(bg.shape, lambda g: (0, 0, 0, 0), pipeline_mode=pl.Buffered(1))],
        out_specs=pl.BlockSpec((vecs, vecs), lambda g: (0, 0)),
        scratch_shapes=[
            pltpu.VMEM((256, 256), BF16),
            pltpu.VMEM((256, 256), BF16),
            pltpu.VMEM((2, 4, cycles, 8, samples), F32),
            pltpu.VMEM((2, cycles, GROUP, samples), F32),
            pltpu.VMEM((2, cycles, GROUP, samples), F32),
            pltpu.VMEM((2, cycles, vecs, samples), BF16),
            pltpu.VMEM((2, cycles, vecs, samples), BF16),
            pltpu.VMEM((2, 2, 8, 128, 256), BF16),
            pltpu.VMEM(bg.shape, F32),
            pltpu.VMEM((vecs, vecs), F32),
            pltpu.VMEM((2,) + block, BF16),
            pltpu.SemaphoreType.DMA((2,)),
        ],
        compiler_params=pltpu.CompilerParams(vmem_limit_bytes=63 * 1024 * 1024),
        name="segment_transfer",
    )(nbr.T, steps, det, disp, basis, bg)


def split2(x):
    hi = x.astype(jnp.bfloat16)
    return hi, (x - hi.astype(jnp.float32)).astype(jnp.bfloat16)


def mm3(a, b):
    ah, al = split2(a)
    bh, bl = split2(b)
    return jnp.dot(jnp.concatenate([ah, ah, al], axis=1), jnp.concatenate([bh, bl, bh], axis=0),
                   preferred_element_type=jnp.float32)


def _chain_kernel(t_ref, ends, slots, pair, low, before, send_sem, recv_sem):
    seq, grp = lax.axis_index("seq"), lax.axis_index("grp")
    core = lax.rem(grp, 2)
    depth = lax.rem(lax.div(grp, 2), 4)
    wide = lax.div(grp, 8)
    rounds = (
        (4, seq, lambda pos: (pos, grp)),
        (2, core, lambda pos: (seq, grp - core + pos)),
        (4, depth, lambda pos: (seq, grp + (pos - depth) * 2)),
        (4, wide, lambda pos: (seq, grp + (pos - wide) * 8)),
    )
    mesh_id = pl.DeviceIdType.MESH
    barrier = pltpu.get_barrier_semaphore()
    for radix, pos, place in rounds:
        for hop in range(1, radix):
            pl.semaphore_signal(barrier, inc=1, device_id=place(lax.rem(pos + hop, radix)), device_id_type=mesh_id)
    pl.semaphore_wait(barrier, sum(r[0] - 1 for r in rounds))

    def prefix_step(k):
        radix, pos, _ = rounds[k]

        @pl.when(pos == 1)
        def _():
            before[...] = slots[k, 0] if k == 0 else mm3(before[...], slots[k, 0])

        if radix == 4:
            @pl.when(pos == 2)
            def _():
                before[...] = low[...] if k == 0 else mm3(before[...], low[...])

            @pl.when(pos == 3)
            def _():
                left = slots[k, 2] if k == 0 else mm3(before[...], slots[k, 2])
                before[...] = mm3(left, low[...])

    n = t_ref.shape[0]
    i = lax.broadcasted_iota(jnp.int32, (n, n), 0)
    j = lax.broadcasted_iota(jnp.int32, (n, n), 1)
    eye = jnp.where(i == j, 1.0, 0.0)
    before[...] = eye
    sends = []
    own = t_ref
    for k, (radix, pos, place) in enumerate(rounds):
        copies = []
        for hop in ((1, 3, 2) if radix == 4 else (1,)):
            copy = pltpu.make_async_remote_copy(
                src_ref=own, dst_ref=slots.at[k, pos], send_sem=send_sem.at[k, hop], recv_sem=recv_sem.at[k, hop],
                device_id=place(lax.rem(pos + hop, radix)), device_id_type=mesh_id)
            copy.start()
            copies.append(copy)
        sends += copies
        slots[k, pos] = own[...]
        if k:
            prefix_step(k - 1)
        for copy in copies:
            copy.wait_recv()
        if k + 1 == len(rounds):
            break
        total = mm3(slots[k, 1], slots[k, 0])
        if radix == 4:
            low[...] = total
            total = mm3(mm3(slots[k, 3], slots[k, 2]), total)
        pair[k] = total
        own = pair.at[k]

    k = len(rounds) - 1
    first = mm3(slots[k, 1], slots[k, 0])
    ends[0] = mm3(slots[k, 3], slots[k, 2])
    ends[1] = first
    ends[2] = before[...]
    ends[3] = first

    @pl.when(wide == 3)
    def _():
        ends[2] = mm3(before[...], slots[k, 2])

    @pl.when(wide == 1)
    def _():
        ends[3] = slots[k, 0]

    @pl.when(wide == 0)
    def _():
        ends[3] = eye

    for copy in sends:
        copy.wait_send()


def _finish_kernel(ends, pre_ref, mono_ref):
    mono_ref[...] = mm3(ends[0], ends[1])
    pre_ref[...] = mm3(ends[2], ends[3])


def chain(t):
    n = t.shape[0]
    shape = jax.ShapeDtypeStruct((n, n), jnp.float32)
    vm = pl.BlockSpec(memory_space=pltpu.VMEM)
    ends = pl.pallas_call(
        _chain_kernel, out_shape=jax.ShapeDtypeStruct((4, n, n), jnp.float32), in_specs=[vm], out_specs=vm,
        scratch_shapes=[pltpu.VMEM((4, 4, n, n), jnp.float32), pltpu.VMEM((3, n, n), jnp.float32),
                        pltpu.VMEM((n, n), jnp.float32), pltpu.VMEM((n, n), jnp.float32),
                        pltpu.SemaphoreType.DMA((4, 4)), pltpu.SemaphoreType.DMA((4, 4))],
        compiler_params=pltpu.CompilerParams(collective_id=0, has_side_effects=True),
        name="chain_products")(t)
    return pl.pallas_call(
        _finish_kernel, out_shape=(shape, shape), in_specs=[vm], out_specs=(vm, vm),
        name="last_products")(ends)

def shards(basis, background, detuning, dispersion, neighbors, step_counts):
    own = segment_transfer(
        basis, background[0, 0], detuning, dispersion, neighbors, step_counts.reshape(1)
    )
    prefix, monodromy = chain(own)
    return (prefix[None, None], monodromy)


def solution(mesh):
    in_specs = (P(), P("grp", "seq", None, None, None, None), P(), P(), P(), P("grp", "seq"))
    out_specs = (P("grp", "seq", None, None), P())
    return jax.shard_map(shards, mesh=mesh, in_specs=in_specs, out_specs=out_specs, check_vma=False)
```
